32 devices in a mesh: groups: 2 (over y), req: 16 (over z, x, core).
Axes of the slice: x: 2, y: 2, z: 4, core: 2. Of those that a mesh axis runs over, the one named last changes fastest.
Arguments:
- kv_cache: bfloat16 [1152, 2, 128, 512], P(('groups', 'req')), parts along dimension 0
- draft_rows: bfloat16 [1536, 5120], P(('groups', 'req')), parts along dimension 0
- cache_lengths: int32 [384], P('groups'), parts along dimension 0, may hold values from 1 to 384, as said below
- row_offsets: int32 [32], P('groups'), parts along dimension 0, may hold values from 0 to 15, as said below
- draft_order: int32 [1536], P(('groups', 'req')), parts along dimension 0, may hold values from 0 to 47, as said below
- pair_mask: int32 [2], P('groups'), parts along dimension 0, may hold values from 1 to 15
- moved_slots: int32 [32], P('groups'), parts along dimension 0, may hold values from 0 to 11
Outputs:
- verified: bfloat16 [1536, 4096], P(('groups', 'req')), parts along dimension 0
The draws below stay inside these ranges and needn't reach their ends.
There are 2 independent parts, one for each index of `groups`. The reference program is written for one: setup_inputs(seed, part) draws one part's arguments, and reference() takes and returns one part's arrays. A program takes and returns all parts, laid end to end along the dimension named above; each array names one. Nothing has to cross between parts.
Inputs may be any that keep to these rules, and one draw needn't show every extreme that they name: `row_offsets`: all entries are different; the offsets 1, 15 and 8 are always among them. `draft_order`: each device's 48 entries are a permutation. `cache_lengths`: some request has exactly 384 positions.
All inputs are finite; a program needn't handle non-finite values.
Results may differ from the reference program's by a relative error of at most 0.0037.
Values may be sent and summed in bfloat16 or wider, within the bound.
No kernel may reach another device: no remote copies, remote signals or barrier semaphores. Data moves between devices by JAX's collectives and lax.ppermute only.
A program may use at most 128 MiB of HBM per device.

```python
import jax
import jax.numpy as jnp
from jax import lax

QH = 32
KVH = 4
HD = 128
DRAFT = 4
PAGE = 128
R_DEV = 12
PPR = 3
LMAX = 384
QW = 4096
KVW = 512
ROW_W = 5120
DR_DEV = 48
CAP = 3
REQS = 192
ROWS = 768
CACHE_PAGES = 576
N_REQ = 16


def draw_kv_cache(key, part):
    values = jax.random.normal(jax.random.fold_in(key, 11), (CACHE_PAGES, 2, PAGE, KVH, HD), jnp.float32)
    return values.reshape(CACHE_PAGES, 2, PAGE, KVW).astype(jnp.bfloat16)


def draw_draft_rows(key, part):
    values = jax.random.normal(jax.random.fold_in(key, 21), (ROWS, ROW_W), jnp.float32)
    return values.astype(jnp.bfloat16)


def draw_cache_lengths(key, part):
    first = jax.random.randint(jax.random.fold_in(key, 31), (REQS,), 0, LMAX)
    second = jax.random.randint(jax.random.fold_in(key, 32), (REQS,), 0, LMAX)
    longest = jax.random.randint(jax.random.fold_in(key, 33), (), 0, REQS)
    lengths = 1 + first * second // LMAX
    return jnp.where(jnp.arange(REQS, dtype=jnp.int32) == longest, LMAX, lengths).astype(jnp.int32)


def draw_row_offsets(key, part):
    order = jax.random.permutation(jax.random.fold_in(key, 41), N_REQ).astype(jnp.int32)
    rank = jnp.argsort(order).astype(jnp.int32)
    values = jnp.arange(N_REQ, dtype=jnp.int32)
    forced = (values == 1) | (values == N_REQ - 1) | (values == N_REQ // 2)
    score = jnp.where(forced, rank - N_REQ, rank)
    chosen = jnp.argsort(score)[:DR_DEV // CAP].astype(jnp.int32)
    return jax.random.permutation(jax.random.fold_in(key, 42), chosen).astype(jnp.int32)


def draw_draft_order(key, part):
    subkeys = jax.random.split(jax.random.fold_in(key, 51), N_REQ)
    orders = jax.vmap(lambda sub: jax.random.permutation(sub, DR_DEV))(subkeys)
    return orders.reshape(ROWS).astype(jnp.int32)


def plant(drawn, rng, smallest, largest):
    longest = drawn.shape.index(max(drawn.shape))
    spots = []
    for shift in (0, 1):
        where = [jax.random.randint(jax.random.fold_in(rng, axis), (), 0, length) for axis, length in enumerate(drawn.shape)]
        where[longest] = (where[longest] + shift) % drawn.shape[longest]
        spots.append(tuple(where))
    return drawn.at[spots[0]].set(smallest).at[spots[1]].set(largest)


def setup_inputs(seed: int = 0, part: int = 0) -> dict:
    arg_keys = jax.random.split(jax.random.key(seed), 8)
    part_keys = jax.random.split(jax.random.fold_in(arg_keys[7], part), 8)
    kv_cache = draw_kv_cache(jax.random.fold_in(jax.random.fold_in(arg_keys[7], part), 71), part)
    draft_rows = draw_draft_rows(jax.random.fold_in(jax.random.fold_in(arg_keys[7], part), 71), part)
    cache_lengths = draw_cache_lengths(jax.random.fold_in(jax.random.fold_in(arg_keys[7], part), 71), part)
    row_offsets = draw_row_offsets(jax.random.fold_in(jax.random.fold_in(arg_keys[7], part), 71), part)
    draft_order = draw_draft_order(jax.random.fold_in(jax.random.fold_in(arg_keys[7], part), 71), part)
    pair_mask = jax.random.randint(part_keys[5], (1,), 1, N_REQ).astype(jnp.int32)
    moved_slots = plant(jax.random.randint(part_keys[6], (N_REQ,), 0, R_DEV), jax.random.fold_in(part_keys[6], 1), 0, R_DEV - 1).astype(jnp.int32)
    return {"kv_cache": kv_cache, "draft_rows": draft_rows, "cache_lengths": cache_lengths, "row_offsets": row_offsets, "draft_order": draft_order, "pair_mask": pair_mask, "moved_slots": moved_slots}


def attend_one(pages, length, row_block):
    grp = QH // KVH
    cache_keys = pages[:, 0].reshape(LMAX, KVH, HD).astype(jnp.float32)
    cache_vals = pages[:, 1].reshape(LMAX, KVH, HD).astype(jnp.float32)
    queries = row_block[:, :QW].reshape(DRAFT, KVH, grp, HD).astype(jnp.float32)
    new_keys = row_block[:, QW:QW + KVW].reshape(DRAFT, KVH, HD).astype(jnp.float32)
    new_vals = row_block[:, QW + KVW:].reshape(DRAFT, KVH, HD).astype(jnp.float32)
    factor = 1.0 / jnp.sqrt(jnp.float32(HD))
    cache_score = jnp.einsum('tghd,lgd->tghl', queries, cache_keys) * factor
    new_score = jnp.einsum('tghd,ugd->tghu', queries, new_keys) * factor
    cache_valid = (jnp.arange(LMAX, dtype=jnp.int32) < length)[None, None, None, :]
    positions = jnp.arange(DRAFT, dtype=jnp.int32)
    new_valid = (positions[None, :] <= positions[:, None])[:, None, None, :]
    cache_score = jnp.where(cache_valid, cache_score, jnp.float32(-1e+30))
    new_score = jnp.where(new_valid, new_score, jnp.float32(-1e+30))
    peak = jnp.maximum(lax.optimization_barrier(jnp.max(cache_score, axis=-1)), lax.optimization_barrier(jnp.max(new_score, axis=-1)))
    cache_weight = jnp.where(cache_valid, jnp.exp(cache_score - peak[..., None]), 0.0)
    new_weight = jnp.where(new_valid, jnp.exp(new_score - peak[..., None]), 0.0)
    denominator = lax.optimization_barrier(jnp.sum(cache_weight, axis=-1)) + lax.optimization_barrier(jnp.sum(new_weight, axis=-1))
    cache_weight = cache_weight.astype(jnp.bfloat16).astype(jnp.float32)
    new_weight = new_weight.astype(jnp.bfloat16).astype(jnp.float32)
    summed = jnp.einsum('tghl,lgd->tghd', cache_weight, cache_vals) + jnp.einsum('tghu,ugd->tghd', new_weight, new_vals)
    return (summed / denominator[..., None]).reshape(DRAFT, QW).astype(jnp.bfloat16)

def reference(kv_cache, draft_rows, cache_lengths, row_offsets, draft_order, pair_mask, moved_slots):
    page_pool = kv_cache.reshape(N_REQ, R_DEV, PPR, 2, PAGE, KVW)
    devices = jnp.arange(N_REQ, dtype=jnp.int32)
    partner = jnp.bitwise_xor(devices, pair_mask[0])
    slot_ids = jnp.arange(R_DEV, dtype=jnp.int32)
    moved_here = slot_ids[None, :] == moved_slots[:, None]
    ident_dev = jnp.where(moved_here, partner[:, None], devices[:, None])
    ident_slot = jnp.where(moved_here, moved_slots[partner][:, None], slot_ids[None, :])
    owner_k = draft_order.reshape(N_REQ, DR_DEV)
    owner_e = (devices[:, None] - row_offsets[owner_k // CAP]) % N_REQ
    owned = jnp.zeros((N_REQ, DR_DEV, ROW_W), jnp.bfloat16)
    owned = owned.at[owner_e.reshape(-1), owner_k.reshape(-1)].set(draft_rows)

    def per_owner(owner):

        def per_slot(slot):
            source_dev = ident_dev[owner, slot]
            source_slot = ident_slot[owner, slot]
            pages = page_pool[source_dev, source_slot]
            length = cache_lengths[source_dev * R_DEV + source_slot]
            row_block = lax.dynamic_slice_in_dim(owned[owner], slot * DRAFT, DRAFT, 0)
            return attend_one(pages, length, row_block)
        return lax.map(per_slot, slot_ids).reshape(DR_DEV, QW)
    owner_out = lax.map(per_owner, devices)
    verified = owner_out[owner_e.reshape(-1), owner_k.reshape(-1)]
    return verified
```

```python
import functools

import jax
import jax.numpy as jnp
from jax import lax
from jax.experimental import pallas as pl
from jax.experimental.pallas import tpu as pltpu
from jax.sharding import PartitionSpec as P

HD = 128
DRAFT = 4
PAGE = 128
R_DEV = 12
PPR = 3
QW = 4096
KVW = 512
KVH = KVW // HD
GRP = QW // KVW
LANES = 128
WIDE = QW // GRP + LANES
SPAN = R_DEV * GRP * DRAFT
SLOT = GRP * DRAFT
BF = jnp.bfloat16
F32 = jnp.float32
I32 = jnp.int32
VMEM = pl.BlockSpec(memory_space=pltpu.VMEM)
SMEM = pl.BlockSpec(memory_space=pltpu.SMEM)


def iota(shape, dim):
    return lax.broadcasted_iota(I32, shape, dim)


def onehot(mask):
    return jnp.where(mask, jnp.float32(1), jnp.float32(0)).astype(BF)


def exact_dot(a, b):
    return jnp.dot(a, b, preferred_element_type=F32)


def stacked(value, cap):
    width = value.shape[1] // cap
    return jnp.concatenate([value[:, r * width : (r + 1) * width] for r in range(cap)], axis=0)


def wrapped(value, count):
    value = jnp.where(value < 0, value + count, value)
    return jnp.where(value >= count, value - count, value)


def peers_of(k, offs_ref, cap, sign, me, count):
    off = jnp.full(k.shape, offs_ref[0], I32)
    first = jnp.zeros(k.shape, I32)
    for i in range(1, offs_ref.shape[0]):
        off = jnp.where(k >= i * cap, offs_ref[i], off)
        first = jnp.where(k >= i * cap, i * cap, first)
    return wrapped(me + sign * off, count), k - first


def pack_kernel(count, cap, order_ref, offs_ref, rows_ref, out_ref, stack_ref):
    rows = rows_ref.shape[0]
    for h in range(GRP):
        for g in range(KVH):
            c = (g * GRP + h) * HD
            stack_ref[h * rows : (h + 1) * rows, g * HD : (g + 1) * HD] = rows_ref[:, c : c + HD]
        c = QW + h * HD
        stack_ref[h * rows : (h + 1) * rows, KVH * HD :] = rows_ref[:, c : c + HD]
    me = lax.axis_index("req")
    k = order_ref[...]
    peer, place = peers_of(k, offs_ref, cap, -1, me, count)
    wide = GRP * rows
    lane = iota((rows, wide), 1)
    tile = functools.reduce(
        jnp.logical_or, [lane == iota((rows, wide), 0) + h * rows for h in range(GRP)]
    )
    tile = onehot(tile)
    peer = exact_dot(jnp.broadcast_to(peer.astype(F32), (8, rows)).astype(BF), tile)[:1]
    place = exact_dot(jnp.broadcast_to(place.astype(F32), (8, rows)).astype(BF), tile)[:1]
    lane = iota((1, wide), 1)
    part = sum([(lane >= h * rows).astype(I32) for h in range(1, GRP)])
    spot = peer.astype(I32) * GRP + part
    at = iota((count * GRP, wide), 0)
    for r in range(cap):
        here = jnp.where(place.astype(I32) == r, spot, -1)
        out_ref[:, r * WIDE : (r + 1) * WIDE] = exact_dot(onehot(at == here), stack_ref[...]).astype(BF)


def visitor_kernel(count, cap, offs_ref, moved_ref, in_ref, out_ref):
    me = lax.axis_index("req")
    slot = moved_ref[me]
    wide = cap * count * GRP
    row = iota((SLOT, wide), 0)
    spot = jnp.zeros((SLOT, wide), I32)
    for t in range(DRAFT):
        k = slot * DRAFT + t
        c = k // cap
        peer = wrapped(me + offs_ref[c], count)
        spot = jnp.where((row & (DRAFT - 1)) == t, (k - c * cap) * (count * GRP) + peer * GRP, spot)
    pick = onehot(iota((SLOT, wide), 1) == spot + (row >> 2))
    out_ref[...] = exact_dot(pick, stacked(in_ref[...], cap)).astype(BF)


def attend_kernel(
    count, cap, offs_ref, moved_ref, lengths_ref, in_ref, visitor_ref, kv_ref, out_ref, answer_ref, rows_ref, sums_ref
):
    me = lax.axis_index("req")
    row = iota((SPAN, LANES), 0)
    k = (row >> 5) * DRAFT + (row & (DRAFT - 1))
    peer, place = peers_of(k, offs_ref, cap, 1, me, count)
    spot = place * (count * GRP) + peer * GRP + ((row >> 2) & (GRP - 1))
    lane = iota((SPAN, LANES), 1)
    blocks = cap * count * GRP // LANES
    pick = jnp.concatenate([onehot(spot - b * LANES == lane) for b in range(blocks)], axis=1)
    rows_ref[...] = exact_dot(pick, stacked(in_ref[...], cap)).astype(BF)
    moved = pl.multiple_of(moved_ref[me] * SLOT, SLOT)
    rows_ref[pl.ds(moved, SLOT), :] = visitor_ref[...]
    row = iota((SPAN, SPAN), 0)
    lane = iota((SPAN, SPAN), 1)
    fresh = R_DEV * DRAFT
    turned = functools.reduce(
        jnp.logical_or,
        [
            (row - s * fresh == (lane >> 5) * DRAFT + (lane & (DRAFT - 1))) & (((lane >> 2) & (GRP - 1)) == s)
            for s in range(GRP)
        ],
    )
    fresh_kv = exact_dot(onehot(turned), rows_ref[:, KVH * HD :]).astype(BF)
    factor = 1.0 / jnp.sqrt(jnp.float32(HD))
    row = iota((SPAN, fresh), 0)
    lane = iota((SPAN, fresh), 1)
    seen = ((row >> 5) == (lane >> 2)) & ((lane & (DRAFT - 1)) <= (row & (DRAFT - 1)))
    position = iota((SLOT, PPR * PAGE), 1)
    contract = (((1,), (1,)), ((), ()))
    for g in range(KVH):
        cols = slice(g * HD, (g + 1) * HD)
        new_keys = fresh_kv[g * fresh : (g + 1) * fresh]
        new_vals = fresh_kv[(KVH + g) * fresh : (KVH + g + 1) * fresh]
        new_score = lax.dot_general(rows_ref[:, cols], new_keys, contract, preferred_element_type=F32) * factor
        new_score = jnp.where(seen, new_score, jnp.float32(-1e30))
        new_peak = jnp.max(new_score, axis=1, keepdims=True)
        for s in range(R_DEV):
            mine = slice(s * SLOT, (s + 1) * SLOT)
            length = lengths_ref[me * R_DEV + s]
            keys = jnp.concatenate([kv_ref[s * PPR + p, 0, :, cols] for p in range(PPR)], axis=0)
            vals = jnp.concatenate([kv_ref[s * PPR + p, 1, :, cols] for p in range(PPR)], axis=0)
            score = lax.dot_general(rows_ref[mine, cols], keys, contract, preferred_element_type=F32) * factor
            score = jnp.where(position < length, score, jnp.float32(-1e30))
            peak = jnp.maximum(jnp.max(score, axis=1, keepdims=True), new_peak[mine])
            weight = jnp.exp(score - peak)
            new_weight = jnp.exp(new_score[mine] - peak)
            total = jnp.sum(weight, axis=1, keepdims=True) + jnp.sum(new_weight, axis=1, keepdims=True)
            summed = exact_dot(weight.astype(BF), vals) + exact_dot(new_weight.astype(BF), new_vals)
            out_ref[mine, cols] = (summed / total).astype(BF)
    answer_ref[...] = out_ref[pl.ds(moved, SLOT), :]


def reply_kernel(count, cap, offs_ref, moved_ref, rows_in_ref, answer_ref, out_ref, rows_ref):
    me = lax.axis_index("req")
    rows_ref[...] = rows_in_ref[...]
    moved = pl.multiple_of(moved_ref[me] * SLOT, SLOT)
    rows_ref[pl.ds(moved, SLOT), :] = answer_ref[...]
    lane = iota((1, SPAN), 1)
    k = (lane >> 5) * DRAFT + (lane & (DRAFT - 1))
    peer, place = peers_of(k, offs_ref, cap, 1, me, count)
    spot = peer * GRP + ((lane >> 2) & (GRP - 1))
    at = iota((count * GRP, SPAN), 0)
    for r in range(cap):
        here = jnp.where(place == r, spot, -1)
        out_ref[:, r * KVW : (r + 1) * KVW] = exact_dot(onehot(at == here), rows_ref[...]).astype(BF)


def finish_kernel(count, cap, order_ref, offs_ref, in_ref, out_ref):
    rows = out_ref.shape[0]
    me = lax.axis_index("req")
    peer, place = peers_of(order_ref[...], offs_ref, cap, -1, me, count)
    spot = place * (count * GRP) + peer * GRP
    same = iota((rows, rows), 0) == iota((rows, rows), 1)
    spot = jnp.sum(jnp.where(same, spot, 0).astype(F32), axis=1, keepdims=True).astype(I32)
    wide = cap * count * GRP
    lane = iota((rows, wide), 1)
    pick = jnp.concatenate([onehot(lane == spot + h) for h in range(GRP)], axis=0)
    result = exact_dot(pick, stacked(in_ref[...], cap)).astype(BF)
    for h in range(GRP):
        for g in range(KVH):
            c = (g * GRP + h) * HD
            out_ref[:, c : c + HD] = result[h * rows : (h + 1) * rows, g * HD : (g + 1) * HD]


def hop(value, mask, count):
    step = 1
    while step < count:
        choices = min(16, count // step)
        digit = jnp.bitwise_and(mask // step, choices - 1)
        only = choices == count
        branches = [
            functools.partial(
                lambda by, v: lax.ppermute(v, "req", [(i, i ^ by) for i in range(count)]), d * step
            )
            for d in range(1, choices)
        ]
        if only:
            value = lax.switch(digit - 1, branches, value)
        else:
            value = lax.switch(digit, [lambda v: v] + branches, value)
        step *= choices
    return value


def on_device(kv_cache, draft_rows, cache_lengths, row_offsets, draft_order, pair_mask, moved_slots):
    count = lax.axis_size("req")
    rows = draft_rows.shape[0]
    cap = max(1, rows // count)
    order = draft_order.reshape(1, rows)
    mask = pair_mask[0]

    def call(kernel, specs, outs, scratch=()):
        return pl.pallas_call(
            functools.partial(kernel, count, cap),
            in_specs=specs,
            out_specs=[VMEM] * len(outs) if len(outs) > 1 else VMEM,
            out_shape=[jax.ShapeDtypeStruct(o, BF) for o in outs] if len(outs) > 1 else jax.ShapeDtypeStruct(outs[0], BF),
            scratch_shapes=[pltpu.VMEM(s, BF) for s in scratch],
        )

    outgoing = call(
        pack_kernel, [VMEM, SMEM, VMEM], [(count * GRP, cap * WIDE)], [(GRP * rows, WIDE)]
    )(order, row_offsets, draft_rows)
    incoming = lax.all_to_all(outgoing, "req", split_axis=0, concat_axis=0, tiled=True)
    visitor = call(visitor_kernel, [SMEM, SMEM, VMEM], [(SLOT, WIDE)])(row_offsets, moved_slots, incoming)
    visitor = hop(visitor, mask, count)
    results, answer = call(
        attend_kernel, [SMEM, SMEM, SMEM, VMEM, VMEM, VMEM], [(SPAN, KVW), (SLOT, KVW)], [(SPAN, WIDE), (8, 128)]
    )(row_offsets, moved_slots, cache_lengths, incoming, visitor, kv_cache)
    answer = hop(answer, mask, count)
    backward = call(reply_kernel, [SMEM, SMEM, VMEM, VMEM], [(count * GRP, cap * KVW)], [(SPAN, KVW)])(
        row_offsets, moved_slots, results, answer
    )
    returned = lax.all_to_all(backward, "req", split_axis=0, concat_axis=0, tiled=True)
    return call(finish_kernel, [VMEM, SMEM, VMEM], [(rows, QW)])(order, row_offsets, returned)


def solution(mesh):
    in_specs = (
        P(("groups", "req"), None, None, None),
        P(("groups", "req"), None),
        P("groups"),
        P("groups"),
        P(("groups", "req")),
        P("groups"),
        P("groups"),
    )
    out_specs = P(("groups", "req"), None)
    return jax.shard_map(
        on_device, mesh=mesh, in_specs=in_specs, out_specs=out_specs, check_vma=False
    )
```

```python
import functools

import jax
import jax.numpy as jnp
from jax import lax
from jax.experimental import pallas as pl
from jax.experimental.pallas import tpu as pltpu
from jax.sharding import PartitionSpec as P

HD = 128
DRAFT = 4
PAGE = 128
R_DEV = 12
PPR = 3
QW = 4096
KVW = 512
KVH = KVW // HD
GRP = QW // KVW
LANES = 128
WIDE = QW // GRP + LANES
SPAN = R_DEV * GRP * DRAFT
SLOT = GRP * DRAFT
LAG = 24
BF = jnp.bfloat16
F32 = jnp.float32
I32 = jnp.int32
VMEM = pl.BlockSpec(memory_space=pltpu.VMEM)
SMEM = pl.BlockSpec(memory_space=pltpu.SMEM)


def iota(shape, dim):
    return lax.broadcasted_iota(I32, shape, dim)


def onehot(mask):
    return jnp.where(mask, jnp.float32(1), jnp.float32(0)).astype(BF)


def exact_dot(a, b):
    return jnp.dot(a, b, preferred_element_type=F32)


def stacked(value, cap):
    width = value.shape[1] // cap
    return jnp.concatenate([value[:, r * width : (r + 1) * width] for r in range(cap)], axis=0)


def wrapped(value, count):
    value = jnp.where(value < 0, value + count, value)
    return jnp.where(value >= count, value - count, value)


def peers_of(k, offs_ref, cap, sign, me, count):
    off = jnp.full(k.shape, offs_ref[0], I32)
    first = jnp.zeros(k.shape, I32)
    for i in range(1, offs_ref.shape[0]):
        off = jnp.where(k >= i * cap, offs_ref[i], off)
        first = jnp.where(k >= i * cap, i * cap, first)
    return wrapped(me + sign * off, count), k - first


def owner_row(index):
    return (index >> 5) * DRAFT + (index & (DRAFT - 1)), (index >> 2) & (GRP - 1)


def pack_kernel(count, cap, order_ref, offs_ref, rows_ref, out_ref, stack_ref):
    rows = rows_ref.shape[0]
    me = lax.axis_index("req")
    peer, place = peers_of(order_ref[...], offs_ref, cap, -1, me, count)
    wide = GRP * rows
    lane = iota((1, wide), 1)
    part = sum([(lane >= h * rows).astype(I32) for h in range(1, GRP)])
    tile = onehot(iota((rows, wide), 0) == lane - part * rows)
    both = jnp.where(iota((8, rows), 0) == 0, peer, place)
    both = exact_dot(both.astype(F32).astype(BF), tile).astype(I32)
    spot = both[:1] * GRP + part
    place = both[1:2]
    for h in range(GRP):
        for g in range(KVH):
            c = (g * GRP + h) * HD
            stack_ref[h * rows : (h + 1) * rows, g * HD : (g + 1) * HD] = rows_ref[:, c : c + HD]
        c = QW + h * HD
        stack_ref[h * rows : (h + 1) * rows, KVH * HD :] = rows_ref[:, c : c + HD]
    at = iota((count * GRP, wide), 0)
    for r in range(cap):
        here = jnp.where(place == r, spot, -1)
        out_ref[:, r * WIDE : (r + 1) * WIDE] = exact_dot(onehot(at == here), stack_ref[...]).astype(BF)


def maps_kernel(
    count,
    cap,
    order_ref,
    offs_ref,
    moved_ref,
    lengths_ref,
    visit_ref,
    take_ref,
    fresh_ref,
    give_ref,
    done_ref,
    limit_ref,
):
    me = lax.axis_index("req")
    moved = moved_ref[me]
    wide = cap * count * GRP
    row = iota((SLOT, wide), 0)
    spot = jnp.zeros((SLOT, wide), I32)
    for t in range(DRAFT):
        k = moved * DRAFT + t
        c = k // cap
        peer = wrapped(me + offs_ref[c], count)
        spot = jnp.where((row & (DRAFT - 1)) == t, (k - c * cap) * (count * GRP) + peer * GRP, spot)
    visit_ref[...] = onehot(iota((SLOT, wide), 1) == spot + (row >> 2))
    row = iota((SPAN, LANES), 0)
    lane = iota((SPAN, LANES), 1)
    fresh = R_DEV * DRAFT
    part = sum([(row >= h * fresh).astype(I32) for h in range(1, GRP)])
    for out, (k, h) in ((take_ref, owner_row(row)), (fresh_ref, (row - part * fresh, part))):
        peer, place = peers_of(k, offs_ref, cap, 1, me, count)
        spot = place * (count * GRP) + peer * GRP + h
        spot = jnp.where((k >> 2) == moved, wide + h * DRAFT + (k & (DRAFT - 1)), spot)
        for b in range(wide // LANES):
            out[:, b * LANES : (b + 1) * LANES] = onehot(spot - b * LANES == lane)
        out[:, wide:] = onehot(spot - wide == lane)[:, :SLOT]
    lane = iota((1, SPAN), 1)
    k, h = owner_row(lane)
    peer, place = peers_of(k, offs_ref, cap, 1, me, count)
    spot = place * (count * GRP) + peer * GRP + h
    at = iota((wide, SPAN), 0)
    give_ref[:, :SPAN] = onehot(at == jnp.where((lane >> 5) == moved, -1, spot))
    lane = iota((1, SLOT), 1)
    spot = jnp.full((1, SLOT), 0, I32)
    for t in range(DRAFT):
        k = moved * DRAFT + t
        c = k // cap
        peer = wrapped(me + offs_ref[c], count)
        spot = jnp.where((lane & (DRAFT - 1)) == t, (k - c * cap) * (count * GRP) + peer * GRP, spot)
    give_ref[:, SPAN:] = onehot(iota((wide, SLOT), 0) == spot + (lane >> 2))
    rows = order_ref.shape[1]
    peer, place = peers_of(order_ref[...], offs_ref, cap, -1, me, count)
    spot = place * (count * GRP) + peer * GRP
    same = iota((rows, rows), 0) == iota((rows, rows), 1)
    spot = jnp.sum(jnp.where(same, spot, 0).astype(F32), axis=1, keepdims=True).astype(I32)
    lane = iota((rows, wide), 1)
    for h in range(GRP):
        done_ref[h * rows : (h + 1) * rows, :] = onehot(lane == spot + h)
    row = iota((16, LANES), 0)
    limit = jnp.full((16, LANES), moved, I32)
    for s in range(R_DEV):
        limit = jnp.where(row == s, lengths_ref[me * R_DEV + s], limit)
    limit_ref[...] = limit


def visitor_kernel(count, cap, visit_ref, in_ref, out_ref):
    out_ref[...] = exact_dot(visit_ref[...], stacked(in_ref[...], cap)).astype(BF)


def attend_kernel(
    count,
    cap,
    take_ref,
    fresh_map_ref,
    limit_ref,
    in_ref,
    visitor_ref,
    cache_ref,
    out_ref,
    answer_ref,
    rows_ref,
    fresh_ref,
    kv_ref,
    score_ref,
    weight_ref,
    inverse_ref,
    sems,
):
    fetches = [
        pltpu.make_async_copy(cache_ref.at[s * PPR : (s + 1) * PPR], kv_ref.at[s * PPR : (s + 1) * PPR], sems.at[s])
        for s in range(R_DEV)
    ]
    for fetch in fetches:
        fetch.start()
    moved = pl.multiple_of(jnp.max(limit_ref[R_DEV : R_DEV + 1, :]) * SLOT, SLOT)
    arrived = jnp.concatenate([stacked(in_ref[...], cap), visitor_ref[...]], axis=0)
    fresh_ref[...] = exact_dot(fresh_map_ref[...], arrived[:, KVW:]).astype(BF)
    rows_ref[...] = exact_dot(take_ref[...], arrived[:, :KVW]).astype(BF)
    fresh = R_DEV * DRAFT
    scale = jnp.float32(HD**-0.5 * 1.4426950408889634)
    span = PPR * PAGE
    contract = (((1,), (1,)), ((), ()))
    position = iota((1, span), 1)
    two = 2 * SLOT
    lane = iota((two, fresh), 1)
    draft = iota((two, fresh), 0) & (DRAFT - 1)
    seen = jnp.where((lane & (DRAFT - 1)) <= draft, lane >> 2, -1)
    low = jnp.float32(-1e30)
    blank = jnp.zeros((SLOT, HD), BF)
    units = [(s, g) for s in range(R_DEV) for g in range(0, KVH, 2)]

    def pair(s, g, kind):
        news = [fresh_ref[(kind * KVH + i) * fresh : (kind * KVH + i + 1) * fresh] for i in (g, g + 1)]
        return jnp.concatenate(
            [kv_ref[s * PPR + p, kind, :, g * HD : (g + 2) * HD] for p in range(PPR)] + [jnp.concatenate(news, axis=1)],
            axis=0,
        )

    def score(u):
        s, g = units[u]
        if g == 0:
            fetches[s].wait()
        mine = slice(s * SLOT, (s + 1) * SLOT)
        first = jnp.concatenate([rows_ref[mine, g * HD : (g + 1) * HD], blank], axis=1)
        second = jnp.concatenate([blank, rows_ref[mine, (g + 1) * HD : (g + 2) * HD]], axis=1)
        queries = jnp.concatenate([first, second], axis=0)
        score_ref[u, :, : span + fresh] = lax.dot_general(
            queries, pair(s, g, 0), contract, preferred_element_type=F32
        )

    def weigh(u):
        s, g = units[u]
        limit = limit_ref[s : s + 1, :]
        limit = jnp.concatenate([limit] * (span // LANES), axis=1)
        old = jnp.where(position < limit, score_ref[u, :, :span], low)
        new = jnp.where(seen == s, score_ref[u, :, span : span + fresh], low)
        peak = jnp.maximum(jnp.max(old, axis=1, keepdims=True), jnp.max(new, axis=1, keepdims=True))
        old = jnp.exp2((old - peak) * scale)
        new = jnp.exp2((new - peak) * scale)
        total = jnp.sum(old, axis=1, keepdims=True) + jnp.sum(new, axis=1, keepdims=True)
        weight_ref[u, :, :span] = old.astype(BF)
        weight_ref[u, :, span : span + fresh] = new.astype(BF)
        inverse_ref[u] = jnp.broadcast_to(1.0 / total, (two, HD))

    def combine(u):
        s, g = units[u]
        mine = slice(s * SLOT, (s + 1) * SLOT)
        summed = exact_dot(weight_ref[u, :, : span + fresh], pair(s, g, 1))
        for i in range(2):
            part = slice(i * SLOT, (i + 1) * SLOT)
            out_ref[mine, (g + i) * HD : (g + i + 1) * HD] = (
                summed[part, i * HD : (i + 1) * HD] * inverse_ref[u, part, :]
            ).astype(BF)

    for i in range(len(units) + LAG + LAG):
        for step, stage in enumerate((score, weigh, combine)):
            if 0 <= i - step * LAG < len(units):
                stage(i - step * LAG)
    answer_ref[...] = out_ref[pl.ds(moved, SLOT), :]


def reply_kernel(count, cap, give_ref, rows_ref, answer_ref, out_ref):
    rows = jnp.concatenate([rows_ref[...], answer_ref[...]], axis=0)
    sent = exact_dot(give_ref[...], rows).astype(BF)
    for r in range(cap):
        out_ref[:, r * KVW : (r + 1) * KVW] = sent[r * count * GRP : (r + 1) * count * GRP]


def finish_kernel(count, cap, done_ref, in_ref, out_ref):
    rows = out_ref.shape[0]
    result = exact_dot(done_ref[...], stacked(in_ref[...], cap)).astype(BF)
    for h in range(GRP):
        for g in range(KVH):
            c = (g * GRP + h) * HD
            out_ref[:, c : c + HD] = result[h * rows : (h + 1) * rows, g * HD : (g + 1) * HD]


def hop(value, mask, count):
    step = 1
    while step < count:
        choices = min(16, count // step)
        digit = jnp.bitwise_and(mask // step, choices - 1)
        only = choices == count
        branches = [
            functools.partial(
                lambda by, v: lax.ppermute(v, "req", [(i, i ^ by) for i in range(count)]), d * step
            )
            for d in range(1, choices)
        ]
        if only:
            value = lax.switch(digit - 1, branches, value)
        else:
            value = lax.switch(digit, [lambda v: v] + branches, value)
        step *= choices
    return value


def on_device(kv_cache, draft_rows, cache_lengths, row_offsets, draft_order, pair_mask, moved_slots):
    count = lax.axis_size("req")
    rows = draft_rows.shape[0]
    cap = max(1, rows // count)
    order = draft_order.reshape(1, rows)
    mask = pair_mask[0]

    def call(kernel, specs, outs, scratch=(), room=8, flops=10**8):
        outs = [o if isinstance(o, jax.ShapeDtypeStruct) else jax.ShapeDtypeStruct(o, BF) for o in outs]
        single = len(outs) == 1
        return pl.pallas_call(
            functools.partial(kernel, count, cap),
            in_specs=specs,
            out_specs=VMEM if single else [VMEM] * len(outs),
            out_shape=outs[0] if single else outs,
            scratch_shapes=[pltpu.VMEM(s, BF) if isinstance(s, tuple) else s for s in scratch],
            compiler_params=pltpu.CompilerParams(vmem_limit_bytes=room * 2**20),
            cost_estimate=pl.CostEstimate(flops=flops, bytes_accessed=10**6, transcendentals=0),
        )

    wide = cap * count * GRP
    outgoing = call(pack_kernel, [VMEM, SMEM, VMEM], [(count * GRP, cap * WIDE)], [(GRP * rows, WIDE)], room=56)(
        order, row_offsets, draft_rows
    )
    incoming = lax.all_to_all(outgoing, "req", split_axis=0, concat_axis=0, tiled=True)
    visit, take, fresh, give, done, limit = call(
        maps_kernel,
        [VMEM, SMEM, SMEM, SMEM],
        [
            (SLOT, wide),
            (SPAN, wide + SLOT),
            (SPAN, wide + SLOT),
            (wide, SPAN + SLOT),
            (GRP * rows, wide),
            jax.ShapeDtypeStruct((16, LANES), I32),
        ],
        room=20,
        flops=10**9,
    )(order, row_offsets, moved_slots, cache_lengths)
    visitor = call(visitor_kernel, [VMEM, VMEM], [(SLOT, WIDE)])(visit, incoming)
    visitor = hop(visitor, mask, count)
    units = R_DEV * KVH // 2
    results, answer = call(
        attend_kernel,
        [VMEM] * 5 + [pl.BlockSpec(memory_space=pltpu.HBM)],
        [(SPAN, KVW), (SLOT, KVW)],
        [
            (SPAN, KVW),
            (SPAN, HD),
            kv_cache.shape,
            pltpu.VMEM((units, 2 * SLOT, (PPR + 1) * PAGE), F32),
            pltpu.VMEM((units, 2 * SLOT, (PPR + 1) * PAGE), BF),
            pltpu.VMEM((units, 2 * SLOT, HD), F32),
            pltpu.SemaphoreType.DMA((R_DEV,)),
        ],
        room=48,
    )(take, fresh, limit, incoming, visitor, kv_cache)
    answer = hop(answer, mask, count)
    backward = call(reply_kernel, [VMEM] * 3, [(count * GRP, cap * KVW)])(give, results, answer)
    returned = lax.all_to_all(backward, "req", split_axis=0, concat_axis=0, tiled=True)
    return call(finish_kernel, [VMEM] * 2, [(rows, QW)])(done, returned)


def solution(mesh):
    in_specs = (
        P(("groups", "req"), None, None, None),
        P(("groups", "req"), None),
        P("groups"),
        P("groups"),
        P(("groups", "req")),
        P("groups"),
        P("groups"),
    )
    out_specs = P(("groups", "req"), None)
    return jax.shard_map(
        on_device, mesh=mesh, in_specs=in_specs, out_specs=out_specs, check_vma=False
    )
```

```python
import functools

import jax
import jax.numpy as jnp
from jax import lax
from jax.experimental import pallas as pl
from jax.experimental.pallas import tpu as pltpu
from jax.sharding import PartitionSpec as P

HD = 128
DRAFT = 4
PAGE = 128
R_DEV = 12
PPR = 3
QW = 4096
KVW = 512
KVH = KVW // HD
GRP = QW // KVW
LANES = 128
WIDE = QW // GRP + LANES
SPAN = R_DEV * GRP * DRAFT
SLOT = GRP * DRAFT
HALF = R_DEV // 2
BODY = 3
ROOM = 16
BF = jnp.bfloat16
F32 = jnp.float32
I32 = jnp.int32
VMEM = pl.BlockSpec(memory_space=pltpu.VMEM)
SMEM = pl.BlockSpec(memory_space=pltpu.SMEM)


def iota(shape, dim):
    return lax.broadcasted_iota(I32, shape, dim)


def onehot(mask):
    return jnp.where(mask, jnp.float32(1), jnp.float32(0)).astype(BF)


def exact_dot(a, b):
    return jnp.dot(a, b, preferred_element_type=F32)


def stacked(value, cap):
    width = value.shape[1] // cap
    return jnp.concatenate([value[:, r * width : (r + 1) * width] for r in range(cap)], axis=0)


def wrapped(value, count):
    value = jnp.where(value < 0, value + count, value)
    return jnp.where(value >= count, value - count, value)


def peers_of(k, offs_ref, cap, sign, me, count):
    off = jnp.full(k.shape, offs_ref[0], I32)
    first = jnp.zeros(k.shape, I32)
    for i in range(1, offs_ref.shape[0]):
        off = jnp.where(k >= i * cap, offs_ref[i], off)
        first = jnp.where(k >= i * cap, i * cap, first)
    return wrapped(me + sign * off, count), k - first


def owner_row(index):
    return (index >> 5) * DRAFT + (index & (DRAFT - 1)), (index >> 2) & (GRP - 1)


def pack_kernel(count, cap, order_ref, offs_ref, rows_ref, out_ref, stack_ref):
    rows = rows_ref.shape[0]
    me = lax.axis_index("req")
    peer, place = peers_of(order_ref[...], offs_ref, cap, -1, me, count)
    wide = GRP * rows
    lane = iota((1, wide), 1)
    part = sum([(lane >= h * rows).astype(I32) for h in range(1, GRP)])
    tile = onehot(iota((rows, wide), 0) == lane - part * rows)
    both = jnp.where(iota((8, rows), 0) == 0, peer, place)
    both = exact_dot(both.astype(F32).astype(BF), tile).astype(I32)
    spot = both[:1] * GRP + part
    place = both[1:2]
    for h in range(GRP):
        for g in range(KVH):
            c = (g * GRP + h) * HD
            stack_ref[h * rows : (h + 1) * rows, g * HD : (g + 1) * HD] = rows_ref[:, c : c + HD]
        c = QW + h * HD
        stack_ref[h * rows : (h + 1) * rows, KVH * HD :] = rows_ref[:, c : c + HD]
    at = iota((count * GRP, wide), 0)
    for r in range(cap):
        here = jnp.where(place == r, spot, -1)
        out_ref[:, r * WIDE : (r + 1) * WIDE] = exact_dot(onehot(at == here), stack_ref[...]).astype(BF)


def maps_kernel(
    count,
    cap,
    order_ref,
    offs_ref,
    moved_ref,
    lengths_ref,
    visit_ref,
    take_ref,
    give_ref,
    done_ref,
    limit_ref,
):
    me = lax.axis_index("req")
    moved = moved_ref[me]
    wide = cap * count * GRP
    row = iota((SLOT, wide), 0)
    spot = jnp.zeros((SLOT, wide), I32)
    for t in range(DRAFT):
        k = moved * DRAFT + t
        c = k // cap
        peer = wrapped(me + offs_ref[c], count)
        spot = jnp.where((row & (DRAFT - 1)) == t, (k - c * cap) * (count * GRP) + peer * GRP, spot)
    visit_ref[...] = onehot(iota((SLOT, wide), 1) == spot + (row >> 2))
    row = iota((SPAN, LANES), 0)
    lane = iota((SPAN, LANES), 1)
    k, h = owner_row(row)
    peer, place = peers_of(k, offs_ref, cap, 1, me, count)
    spot = place * (count * GRP) + peer * GRP + h
    for b in range(wide // LANES):
        take_ref[:, b * LANES : (b + 1) * LANES] = onehot(spot - b * LANES == lane)
    lane = iota((1, SPAN), 1)
    k, h = owner_row(lane)
    peer, place = peers_of(k, offs_ref, cap, 1, me, count)
    spot = place * (count * GRP) + peer * GRP + h
    at = iota((wide, SPAN), 0)
    give_ref[:, :SPAN] = onehot(at == jnp.where((lane >> 5) == moved, -1, spot))
    lane = iota((1, SLOT), 1)
    spot = jnp.full((1, SLOT), 0, I32)
    for t in range(DRAFT):
        k = moved * DRAFT + t
        c = k // cap
        peer = wrapped(me + offs_ref[c], count)
        spot = jnp.where((lane & (DRAFT - 1)) == t, (k - c * cap) * (count * GRP) + peer * GRP, spot)
    give_ref[:, SPAN:] = onehot(iota((wide, SLOT), 0) == spot + (lane >> 2))
    rows = order_ref.shape[1]
    peer, place = peers_of(order_ref[...], offs_ref, cap, -1, me, count)
    spot = place * (count * GRP) + peer * GRP
    same = iota((rows, rows), 0) == iota((rows, rows), 1)
    spot = jnp.sum(jnp.where(same, spot, 0).astype(F32), axis=1, keepdims=True).astype(I32)
    lane = iota((rows, wide), 1)
    for h in range(GRP):
        done_ref[h * rows : (h + 1) * rows, :] = onehot(lane == spot + h)
    row = iota((16, LANES), 0)
    limit = jnp.full((16, LANES), moved, I32)
    limit = jnp.where(row == R_DEV + 1, lengths_ref[me * R_DEV + moved], limit)
    for s in range(R_DEV):
        limit = jnp.where(row == s, lengths_ref[me * R_DEV + s], limit)
    limit_ref[...] = limit


def visitor_kernel(count, cap, visit_ref, in_ref, out_ref):
    out_ref[...] = exact_dot(visit_ref[...], stacked(in_ref[...], cap)).astype(BF)


def attend(slots, rows_of, pages_of, limit_of, put, score_ref, weight_ref, inverse_ref):
    span = PPR * PAGE
    fresh = KVH * DRAFT
    two = 2 * SLOT
    scale = jnp.float32(HD**-0.5 * 1.4426950408889634)
    low = jnp.float32(-1e30)
    position = iota((1, span), 1)
    lane = iota((two, fresh), 1)
    row = iota((two, fresh), 0)
    seen = jnp.where((lane & (DRAFT - 1)) <= (row & (DRAFT - 1)), (lane >> 2) - (row >> 5), -1)
    blank = jnp.zeros((SLOT, HD), BF)
    units = [(s, g) for s in slots for g in range(0, KVH, 2)]

    def pair(s, g, kind):
        new = rows_of(s)[kind * fresh : (kind + 1) * fresh, KVW:]
        pages = [pages_of(s, p, kind, slice(g * HD, (g + 2) * HD)) for p in range(PPR)]
        return jnp.concatenate(pages + [jnp.concatenate([new, new], axis=1)], axis=0)

    def score(u):
        s, g = units[u]
        rows = rows_of(s)
        first = jnp.concatenate([rows[:, g * HD : (g + 1) * HD], blank], axis=1)
        second = jnp.concatenate([blank, rows[:, (g + 1) * HD : (g + 2) * HD]], axis=1)
        score_ref[u, :, : span + fresh] = lax.dot_general(
            jnp.concatenate([first, second], axis=0),
            pair(s, g, 0),
            (((1,), (1,)), ((), ())),
            preferred_element_type=F32,
        )

    def weigh(u):
        s, g = units[u]
        limit = jnp.concatenate([limit_of(s)] * (span // LANES), axis=1)
        old = jnp.where(position < limit, score_ref[u, :, :span], low)
        new = jnp.where(seen == g, score_ref[u, :, span : span + fresh], low)
        peak = jnp.maximum(jnp.max(old, axis=1, keepdims=True), jnp.max(new, axis=1, keepdims=True))
        old = jnp.exp2((old - peak) * scale)
        new = jnp.exp2((new - peak) * scale)
        total = jnp.sum(old, axis=1, keepdims=True) + jnp.sum(new, axis=1, keepdims=True)
        weight_ref[u, :, :span] = old.astype(BF)
        weight_ref[u, :, span : span + fresh] = new.astype(BF)
        inverse_ref[u] = jnp.broadcast_to(1.0 / total, (two, HD))

    def combine(u):
        s, g = units[u]
        summed = exact_dot(weight_ref[u, :, : span + fresh], pair(s, g, 1))
        for i in range(2):
            part = slice(i * SLOT, (i + 1) * SLOT)
            put(s, g + i, (summed[part, i * HD : (i + 1) * HD] * inverse_ref[u, part, :]).astype(BF))

    for stage in (score, weigh, combine):
        for u in range(len(units)):
            stage(u)


def attend_half(low, rows_ref, pages_ref, limit_ref, out_ref, scratch, ready=lambda s: None):
    def step(i, carry):
        slots = [i * BODY + j for j in range(BODY)]
        for s in slots:
            ready(s)

        def put(s, g, value):
            out_ref[pl.ds(pl.multiple_of(s * SLOT, SLOT), SLOT), g * HD : (g + 1) * HD] = value

        attend(
            slots,
            lambda s: rows_ref[pl.ds(pl.multiple_of((s + low) * SLOT, SLOT), SLOT), :],
            lambda s, p, kind, cols: pages_ref[s * PPR + p, kind, :, cols],
            lambda s: limit_ref[pl.ds(s + low, 1), :],
            put,
            *scratch,
        )
        return carry

    lax.fori_loop(0, HALF // BODY, step, 0)


def first_kernel(count, cap, take_ref, limit_ref, in_ref, cache_ref, out_ref, rows_ref, pages_ref, sems, *scratch):
    def fetch(s):
        return pltpu.make_async_copy(cache_ref.at[pl.ds(s * PPR, PPR)], pages_ref.at[pl.ds(s * PPR, PPR)], sems.at[s])

    for s in range(HALF):
        fetch(s).start()
    rows_ref[...] = exact_dot(take_ref[...], stacked(in_ref[...], cap)).astype(BF)
    attend_half(0, rows_ref, pages_ref, limit_ref, out_ref, scratch, lambda s: fetch(s).wait())


def second_kernel(count, cap, rows_ref, limit_ref, answer_ref, cache_ref, out_ref, *scratch):
    attend_half(HALF, rows_ref, cache_ref.at[pl.ds(HALF * PPR, HALF * PPR)], limit_ref, out_ref, scratch)


def guest_kernel(count, cap, visitor_ref, limit_ref, cache_ref, out_ref, *scratch):
    moved = jnp.max(limit_ref[R_DEV : R_DEV + 1, :])

    def put(s, g, value):
        out_ref[:, g * HD : (g + 1) * HD] = value

    attend(
        [moved],
        lambda s: visitor_ref[...],
        lambda s, p, kind, cols: cache_ref[s * PPR + p, kind, :, cols],
        lambda s: limit_ref[R_DEV + 1 : R_DEV + 2, :],
        put,
        *scratch,
    )


def reply_kernel(count, cap, give_ref, first_ref, second_ref, answer_ref, out_ref):
    rows = jnp.concatenate([first_ref[...], second_ref[...], answer_ref[...]], axis=0)
    sent = exact_dot(give_ref[...], rows).astype(BF)
    for r in range(cap):
        out_ref[:, r * KVW : (r + 1) * KVW] = sent[r * count * GRP : (r + 1) * count * GRP]


def finish_kernel(count, cap, done_ref, in_ref, out_ref):
    rows = out_ref.shape[0]
    result = exact_dot(done_ref[...], stacked(in_ref[...], cap)).astype(BF)
    for h in range(GRP):
        for g in range(KVH):
            c = (g * GRP + h) * HD
            out_ref[:, c : c + HD] = result[h * rows : (h + 1) * rows, g * HD : (g + 1) * HD]


def through_partner(mask, count, work, *args):
    def permuted(by, value):
        return lax.ppermute(value, "req", [(i, i ^ by) for i in range(count)])

    if count <= 16:
        branches = [
            functools.partial(lambda by, *a: work(functools.partial(permuted, by), *a), by) for by in range(1, count)
        ]
        return lax.switch(mask - 1, branches, *args)

    def swap(value):
        step = 1
        while step < count:
            choices = min(16, count // step)
            branches = [lambda v: v] + [functools.partial(permuted, d * step) for d in range(1, choices)]
            value = lax.switch(jnp.bitwise_and(mask // step, choices - 1), branches, value)
            step *= choices
        return value

    return work(swap, *args)


def on_device(kv_cache, draft_rows, cache_lengths, row_offsets, draft_order, pair_mask, moved_slots):
    count = lax.axis_size("req")
    rows = draft_rows.shape[0]
    cap = max(1, rows // count)
    order = draft_order.reshape(1, rows)
    mask = pair_mask[0]

    def call(kernel, specs, outs, scratch=(), room=8, flops=10**8):
        outs = [o if isinstance(o, jax.ShapeDtypeStruct) else jax.ShapeDtypeStruct(o, BF) for o in outs]
        single = len(outs) == 1
        return pl.pallas_call(
            functools.partial(kernel, count, cap),
            in_specs=specs,
            out_specs=VMEM if single else [VMEM] * len(outs),
            out_shape=outs[0] if single else outs,
            scratch_shapes=[pltpu.VMEM(s, BF) if isinstance(s, tuple) else s for s in scratch],
            compiler_params=pltpu.CompilerParams(vmem_limit_bytes=room * 2**20),
            cost_estimate=pl.CostEstimate(flops=flops, bytes_accessed=10**6, transcendentals=0),
        )

    wide = cap * count * GRP
    outgoing = call(pack_kernel, [VMEM, SMEM, VMEM], [(count * GRP, cap * WIDE)], [(GRP * rows, WIDE)], room=56)(
        order, row_offsets, draft_rows
    )
    incoming = lax.all_to_all(outgoing, "req", split_axis=0, concat_axis=0, tiled=True)
    visit, take, give, done, limit = call(
        maps_kernel,
        [VMEM, SMEM, SMEM, SMEM],
        [
            (SLOT, wide),
            (SPAN, wide),
            (wide, SPAN + SLOT),
            (GRP * rows, wide),
            jax.ShapeDtypeStruct((16, LANES), I32),
        ],
        room=20,
        flops=10**9,
    )(order, row_offsets, moved_slots, cache_lengths)
    visitor = call(visitor_kernel, [VMEM, VMEM], [(SLOT, WIDE)])(visit, incoming)
    def units(slots):
        return [
            pltpu.VMEM((slots * KVH // 2, 2 * SLOT, (PPR + 1) * PAGE), F32),
            pltpu.VMEM((slots * KVH // 2, 2 * SLOT, (PPR + 1) * PAGE), BF),
            pltpu.VMEM((slots * KVH // 2, 2 * SLOT, HD), F32),
        ]

    hbm = pl.BlockSpec(memory_space=pltpu.HBM)
    pages = (HALF * PPR,) + kv_cache.shape[1:]

    def work(swap, visitor, take, give, limit, incoming, kv_cache):
        arrived = swap(visitor)
        first, owned = call(
            first_kernel,
            [VMEM] * 3 + [hbm],
            [(HALF * SLOT, KVW), (SPAN, WIDE)],
            [pages, pltpu.SemaphoreType.DMA((HALF,))] + units(BODY),
            room=ROOM,
            flops=2 * 10**9,
        )(take, limit, incoming, kv_cache)
        answer = call(guest_kernel, [VMEM] * 3, [(SLOT, KVW)], units(1), room=16)(arrived, limit, kv_cache)
        second = call(
            second_kernel, [VMEM] * 4, [(HALF * SLOT, KVW)], units(BODY), room=16, flops=2 * 10**9
        )(owned, limit, answer, kv_cache)
        answer = swap(answer)
        return call(reply_kernel, [VMEM] * 4, [(count * GRP, cap * KVW)])(give, first, second, answer)

    backward = through_partner(mask, count, work, visitor, take, give, limit, incoming, kv_cache)
    returned = lax.all_to_all(backward, "req", split_axis=0, concat_axis=0, tiled=True)
    return call(finish_kernel, [VMEM] * 2, [(rows, QW)])(done, returned)


def solution(mesh):
    in_specs = (
        P(("groups", "req"), None, None, None),
        P(("groups", "req"), None),
        P("groups"),
        P("groups"),
        P(("groups", "req")),
        P("groups"),
        P("groups"),
    )
    out_specs = P(("groups", "req"), None)
    return jax.shard_map(
        on_device, mesh=mesh, in_specs=in_specs, out_specs=out_specs, check_vma=False
    )
```

```python
import functools

import jax
import jax.numpy as jnp
from jax import lax
from jax.experimental import pallas as pl
from jax.experimental.pallas import tpu as pltpu
from jax.sharding import PartitionSpec as P

HD = 128
DRAFT = 4
PAGE = 128
R_DEV = 12
PPR = 3
QW = 4096
KVW = 512
KVH = KVW // HD
GRP = QW // KVW
LANES = 128
WIDE = QW // GRP + LANES
SPAN = R_DEV * GRP * DRAFT
SLOT = GRP * DRAFT
HALF = R_DEV // 2
BODY = 2
ROOM = 48
BF = jnp.bfloat16
F32 = jnp.float32
I32 = jnp.int32
VMEM = pl.BlockSpec(memory_space=pltpu.VMEM)
SMEM = pl.BlockSpec(memory_space=pltpu.SMEM)


def iota(shape, dim):
    return lax.broadcasted_iota(I32, shape, dim)


def onehot(mask):
    return jnp.where(mask, jnp.float32(1), jnp.float32(0)).astype(BF)


def exact_dot(a, b):
    return jnp.dot(a, b, preferred_element_type=F32)


def stacked(value, cap):
    width = value.shape[1] // cap
    return jnp.concatenate([value[:, r * width : (r + 1) * width] for r in range(cap)], axis=0)


def wrapped(value, count):
    value = jnp.where(value < 0, value + count, value)
    return jnp.where(value >= count, value - count, value)


def peers_of(k, offs_ref, cap, sign, me, count):
    off = jnp.full(k.shape, offs_ref[0], I32)
    first = jnp.zeros(k.shape, I32)
    for i in range(1, offs_ref.shape[0]):
        off = jnp.where(k >= i * cap, offs_ref[i], off)
        first = jnp.where(k >= i * cap, i * cap, first)
    return wrapped(me + sign * off, count), k - first


def owner_row(index):
    return (index >> 5) * DRAFT + (index & (DRAFT - 1)), (index >> 2) & (GRP - 1)


def pack_kernel(
    count, cap, order_hbm, offs_hbm, rows_hbm, out_hbm, order_ref, offs_ref, rows_ref, stack_ref, pick_ref, out_ref, in_sems, out_sems
):
    reads = [
        pltpu.make_async_copy(src, dst, in_sems.at[i])
        for i, (src, dst) in enumerate([(order_hbm, order_ref), (offs_hbm, offs_ref), (rows_hbm, rows_ref)])
    ]
    for read in reads:
        read.start()
    rows = rows_ref.shape[0]
    step = 64
    me = lax.axis_index("req")
    gap = jnp.zeros((step - rows, WIDE), BF)
    for h in range(GRP):
        stack_ref[h * step + rows : (h + 1) * step, :] = gap
    for read in reads[:2]:
        read.wait()
    rest = jnp.full((1, step - rows), -1, I32)
    k = jnp.concatenate([order_ref[...], rest, order_ref[...], rest], axis=1)
    peer, place = peers_of(k, offs_ref, cap, -1, me, count)
    spot = peer * GRP + (iota((1, LANES), 1) >= step).astype(I32)
    spot = jnp.where(k < 0, -1, spot + place * (count * GRP))
    at = iota((cap * count * GRP, LANES), 0)
    for b in range(GRP * step // LANES):
        pick_ref[:, b * LANES : (b + 1) * LANES] = onehot(at - 2 * b == spot)
    reads[2].wait()
    for h in range(GRP):
        for g in range(KVH):
            c = (g * GRP + h) * HD
            stack_ref[h * step : h * step + rows, g * HD : (g + 1) * HD] = rows_ref[:, c : c + HD]
        c = QW + h * HD
        stack_ref[h * step : h * step + rows, KVH * HD :] = rows_ref[:, c : c + HD]
    writes = []
    for start in range(0, WIDE, 2 * LANES):
        size = min(2 * LANES, WIDE - start)
        chunk = exact_dot(pick_ref[...], stack_ref[:, start : start + size]).astype(BF)
        for r in range(cap):
            cols = pl.ds(r * WIDE + start, size)
            out_ref[:, r * WIDE + start : r * WIDE + start + size] = chunk[r * count * GRP : (r + 1) * count * GRP]
            writes.append(pltpu.make_async_copy(out_ref.at[:, cols], out_hbm.at[:, cols], out_sems.at[len(writes)]))
            writes[-1].start()
    for write in writes:
        write.wait()


def maps_kernel(
    count,
    cap,
    order_ref,
    offs_ref,
    moved_ref,
    lengths_ref,
    visit_ref,
    take_ref,
    give_ref,
    done_ref,
    limit_ref,
):
    me = lax.axis_index("req")
    moved = moved_ref[me]
    wide = cap * count * GRP
    row = iota((SLOT, wide), 0)
    spot = jnp.zeros((SLOT, wide), I32)
    for t in range(DRAFT):
        k = moved * DRAFT + t
        c = k // cap
        peer = wrapped(me + offs_ref[c], count)
        spot = jnp.where((row & (DRAFT - 1)) == t, (k - c * cap) * (count * GRP) + peer * GRP, spot)
    visit_ref[...] = onehot(iota((SLOT, wide), 1) == spot + (row >> 2))
    row = iota((SPAN, LANES), 0)
    lane = iota((SPAN, LANES), 1)
    k, h = owner_row(row)
    peer, place = peers_of(k, offs_ref, cap, 1, me, count)
    spot = place * (count * GRP) + peer * GRP + h
    for b in range(wide // LANES):
        take_ref[:, b * LANES : (b + 1) * LANES] = onehot(spot - b * LANES == lane)
    lane = iota((1, SPAN), 1)
    k, h = owner_row(lane)
    peer, place = peers_of(k, offs_ref, cap, 1, me, count)
    spot = place * (count * GRP) + peer * GRP + h
    at = iota((wide, SPAN), 0)
    give_ref[:, :SPAN] = onehot(at == jnp.where((lane >> 5) == moved, -1, spot))
    lane = iota((1, SLOT), 1)
    spot = jnp.full((1, SLOT), 0, I32)
    for t in range(DRAFT):
        k = moved * DRAFT + t
        c = k // cap
        peer = wrapped(me + offs_ref[c], count)
        spot = jnp.where((lane & (DRAFT - 1)) == t, (k - c * cap) * (count * GRP) + peer * GRP, spot)
    give_ref[:, SPAN:] = onehot(iota((wide, SLOT), 0) == spot + (lane >> 2))
    rows = order_ref.shape[1]
    peer, place = peers_of(order_ref[...], offs_ref, cap, -1, me, count)
    spot = place * (count * GRP) + peer * GRP
    same = iota((rows, rows), 0) == iota((rows, rows), 1)
    spot = jnp.sum(jnp.where(same, spot, 0).astype(F32), axis=1, keepdims=True).astype(I32)
    lane = iota((rows, wide), 1)
    for h in range(GRP):
        done_ref[h * rows : (h + 1) * rows, :] = onehot(lane == spot + h)
    row = iota((16, LANES), 0)
    limit = jnp.full((16, LANES), moved, I32)
    limit = jnp.where(row == R_DEV + 1, lengths_ref[me * R_DEV + moved], limit)
    for s in range(R_DEV):
        limit = jnp.where(row == s, lengths_ref[me * R_DEV + s], limit)
    limit_ref[...] = limit


def visitor_kernel(count, cap, visit_ref, in_ref, out_ref):
    out_ref[...] = exact_dot(visit_ref[...], stacked(in_ref[...], cap)).astype(BF)


def attend(slots, rows_of, pages_of, limit_of, put, score_ref, weight_ref, inverse_ref):
    span = PPR * PAGE
    fresh = KVH * DRAFT
    two = 2 * SLOT
    scale = jnp.float32(HD**-0.5 * 1.4426950408889634)
    low = jnp.float32(-1e30)
    position = iota((1, span), 1)
    lane = iota((two, fresh), 1)
    row = iota((two, fresh), 0)
    seen = jnp.where((lane & (DRAFT - 1)) <= (row & (DRAFT - 1)), (lane >> 2) - (row >> 5), -1)
    blank = jnp.zeros((SLOT, HD), BF)
    units = [(s, g) for s in slots for g in range(0, KVH, 2)]

    def pair(s, g, kind):
        new = rows_of(s)[kind * fresh : (kind + 1) * fresh, KVW:]
        pages = [pages_of(s, p, kind, slice(g * HD, (g + 2) * HD)) for p in range(PPR)]
        return jnp.concatenate(pages + [jnp.concatenate([new, new], axis=1)], axis=0)

    def score(u):
        s, g = units[u]
        rows = rows_of(s)
        first = jnp.concatenate([rows[:, g * HD : (g + 1) * HD], blank], axis=1)
        second = jnp.concatenate([blank, rows[:, (g + 1) * HD : (g + 2) * HD]], axis=1)
        score_ref[u, :, : span + fresh] = lax.dot_general(
            jnp.concatenate([first, second], axis=0),
            pair(s, g, 0),
            (((1,), (1,)), ((), ())),
            preferred_element_type=F32,
        )

    def weigh(u):
        s, g = units[u]
        limit = jnp.concatenate([limit_of(s)] * (span // LANES), axis=1)
        old = jnp.where(position < limit, score_ref[u, :, :span], low)
        new = jnp.where(seen == g, score_ref[u, :, span : span + fresh], low)
        peak = jnp.maximum(jnp.max(old, axis=1, keepdims=True), jnp.max(new, axis=1, keepdims=True))
        old = jnp.exp2((old - peak) * scale)
        new = jnp.exp2((new - peak) * scale)
        total = jnp.sum(old, axis=1, keepdims=True) + jnp.sum(new, axis=1, keepdims=True)
        weight_ref[u, :, :span] = old.astype(BF)
        weight_ref[u, :, span : span + fresh] = new.astype(BF)
        inverse_ref[u] = jnp.broadcast_to(1.0 / total, (two, HD))

    def combine(u):
        s, g = units[u]
        summed = exact_dot(weight_ref[u, :, : span + fresh], pair(s, g, 1))
        for i in range(2):
            part = slice(i * SLOT, (i + 1) * SLOT)
            put(s, g + i, (summed[part, i * HD : (i + 1) * HD] * inverse_ref[u, part, :]).astype(BF))

    for stage in (score, weigh, combine):
        for u in range(len(units)):
            stage(u)


def attend_half(low, rows_ref, pages_ref, limit_ref, out_ref, scratch, ready=lambda s: None):
    def step(i, carry):
        slots = [i * BODY + j for j in range(BODY)]
        for s in slots:
            ready(s)

        def put(s, g, value):
            out_ref[pl.ds(pl.multiple_of(s * SLOT, SLOT), SLOT), g * HD : (g + 1) * HD] = value

        attend(
            slots,
            lambda s: rows_ref[pl.ds(pl.multiple_of((s + low) * SLOT, SLOT), SLOT), :],
            lambda s, p, kind, cols: pages_ref[s * PPR + p, kind, :, cols],
            lambda s: limit_ref[pl.ds(s + low, 1), :],
            put,
            *scratch,
        )
        return carry

    lax.fori_loop(0, HALF // BODY, step, 0)


def first_kernel(
    count, cap, take_ref, limit_ref, in_ref, cache_ref, out_ref, rows_ref, guest_ref, later_ref, pages_ref, sems, *scratch
):
    def fetch(s):
        return pltpu.make_async_copy(cache_ref.at[pl.ds(s * PPR, PPR)], pages_ref.at[pl.ds(s * PPR, PPR)], sems.at[s])

    for s in range(HALF):
        fetch(s).start()
    moved = jnp.max(limit_ref[R_DEV : R_DEV + 1, :])
    others = [
        pltpu.make_async_copy(cache_ref.at[pl.ds(moved * PPR, PPR)], guest_ref, sems.at[HALF]),
        pltpu.make_async_copy(cache_ref.at[pl.ds(HALF * PPR, HALF * PPR)], later_ref, sems.at[HALF + 1]),
    ]
    for other in others:
        other.start()
    rows_ref[...] = exact_dot(take_ref[...], stacked(in_ref[...], cap)).astype(BF)
    attend_half(0, rows_ref, pages_ref, limit_ref, out_ref, scratch, lambda s: fetch(s).wait())
    for other in others:
        other.wait()


def second_kernel(count, cap, rows_ref, limit_ref, answer_ref, pages_ref, out_ref, *scratch):
    attend_half(HALF, rows_ref, pages_ref, limit_ref, out_ref, scratch)


def guest_kernel(count, cap, visitor_ref, limit_ref, pages_ref, out_ref, *scratch):
    def put(s, g, value):
        out_ref[:, g * HD : (g + 1) * HD] = value

    attend(
        [0],
        lambda s: visitor_ref[...],
        lambda s, p, kind, cols: pages_ref[p, kind, :, cols],
        lambda s: limit_ref[R_DEV + 1 : R_DEV + 2, :],
        put,
        *scratch,
    )


def reply_kernel(count, cap, give_ref, first_ref, second_ref, answer_ref, out_ref):
    rows = jnp.concatenate([first_ref[...], second_ref[...], answer_ref[...]], axis=0)
    sent = exact_dot(give_ref[...], rows).astype(BF)
    for r in range(cap):
        out_ref[:, r * KVW : (r + 1) * KVW] = sent[r * count * GRP : (r + 1) * count * GRP]


def finish_kernel(count, cap, done_ref, in_ref, out_hbm, out_ref, sems):
    rows = out_ref.shape[0]
    half = GRP // 2
    rhs = stacked(in_ref[...], cap)
    writes = []
    for i in range(2):
        result = exact_dot(done_ref[i * half * rows : (i + 1) * half * rows, :], rhs).astype(BF)
        for h in range(half):
            for g in range(KVH):
                c = (g * GRP + i * half + h) * HD
                out_ref[:, c : c + HD] = result[h * rows : (h + 1) * rows, g * HD : (g + 1) * HD]
        for g in range(KVH):
            cols = pl.ds((g * GRP + i * half) * HD, half * HD)
            writes.append(pltpu.make_async_copy(out_ref.at[:, cols], out_hbm.at[:, cols], sems.at[i * KVH + g]))
            writes[-1].start()
    for write in writes:
        write.wait()


def through_partner(mask, count, work, *args):
    def permuted(by, value):
        return lax.ppermute(value, "req", [(i, i ^ by) for i in range(count)])

    if count <= 16:
        branches = [
            functools.partial(lambda by, *a: work(functools.partial(permuted, by), *a), by) for by in range(1, count)
        ]
        return lax.switch(mask - 1, branches, *args)

    def swap(value):
        step = 1
        while step < count:
            choices = min(16, count // step)
            branches = [lambda v: v] + [functools.partial(permuted, d * step) for d in range(1, choices)]
            value = lax.switch(jnp.bitwise_and(mask // step, choices - 1), branches, value)
            step *= choices
        return value

    return work(swap, *args)


def on_device(kv_cache, draft_rows, cache_lengths, row_offsets, draft_order, pair_mask, moved_slots):
    count = lax.axis_size("req")
    rows = draft_rows.shape[0]
    cap = max(1, rows // count)
    order = draft_order.reshape(1, rows)
    mask = pair_mask[0]

    anywhere = pl.BlockSpec(memory_space=pl.ANY)

    def call(kernel, specs, outs, scratch=(), room=8, flops=10**8, out_spec=VMEM):
        outs = [o if isinstance(o, jax.ShapeDtypeStruct) else jax.ShapeDtypeStruct(o, BF) for o in outs]
        single = len(outs) == 1
        return pl.pallas_call(
            functools.partial(kernel, count, cap),
            in_specs=specs,
            out_specs=out_spec if single else [out_spec] * len(outs),
            out_shape=outs[0] if single else outs,
            scratch_shapes=[pltpu.VMEM(s, BF) if isinstance(s, tuple) else s for s in scratch],
            compiler_params=pltpu.CompilerParams(vmem_limit_bytes=room * 2**20),
            cost_estimate=pl.CostEstimate(flops=flops, bytes_accessed=10**6, transcendentals=0),
        )

    wide = cap * count * GRP
    outgoing = call(
        pack_kernel,
        [anywhere] * 3,
        [(count * GRP, cap * WIDE)],
        [
            pltpu.VMEM((1, rows), I32),
            pltpu.SMEM(row_offsets.shape, I32),
            (rows, draft_rows.shape[1]),
            (GRP * 64, WIDE),
            (cap * count * GRP, GRP * 64),
            (count * GRP, cap * WIDE),
            pltpu.SemaphoreType.DMA((3,)),
            pltpu.SemaphoreType.DMA((cap * pl.cdiv(WIDE, 2 * LANES),)),
        ],
        room=56,
        out_spec=anywhere,
    )(order, row_offsets, draft_rows)
    incoming = lax.all_to_all(outgoing, "req", split_axis=0, concat_axis=0, tiled=True)
    visit, take, give, done, limit = call(
        maps_kernel,
        [VMEM, SMEM, SMEM, SMEM],
        [
            (SLOT, wide),
            (SPAN, wide),
            (wide, SPAN + SLOT),
            (GRP * rows, wide),
            jax.ShapeDtypeStruct((16, LANES), I32),
        ],
        room=20,
        flops=10**9,
    )(order, row_offsets, moved_slots, cache_lengths)
    visitor = call(visitor_kernel, [VMEM, VMEM], [(SLOT, WIDE)])(visit, incoming)
    def units(slots):
        return [
            pltpu.VMEM((slots * KVH // 2, 2 * SLOT, (PPR + 1) * PAGE), F32),
            pltpu.VMEM((slots * KVH // 2, 2 * SLOT, (PPR + 1) * PAGE), BF),
            pltpu.VMEM((slots * KVH // 2, 2 * SLOT, HD), F32),
        ]

    pages = (HALF * PPR,) + kv_cache.shape[1:]

    def work(swap, visitor, take, give, limit, incoming, kv_cache):
        arrived = swap(visitor)
        first, owned, guest, later = call(
            first_kernel,
            [VMEM] * 3 + [anywhere],
            [(HALF * SLOT, KVW), (SPAN, WIDE), (PPR,) + kv_cache.shape[1:], pages],
            [pages, pltpu.SemaphoreType.DMA((HALF + 2,))] + units(BODY),
            room=ROOM,
            flops=2 * 10**9,
        )(take, limit, incoming, kv_cache)
        answer = call(guest_kernel, [VMEM] * 3, [(SLOT, KVW)], units(1), room=8)(arrived, limit, guest)
        second = call(
            second_kernel, [VMEM] * 4, [(HALF * SLOT, KVW)], units(BODY), room=8, flops=2 * 10**9
        )(owned, limit, answer, later)
        answer = swap(answer)
        return call(reply_kernel, [VMEM] * 4, [(count * GRP, cap * KVW)])(give, first, second, answer)

    backward = through_partner(mask, count, work, visitor, take, give, limit, incoming, kv_cache)
    returned = lax.all_to_all(backward, "req", split_axis=0, concat_axis=0, tiled=True)
    return call(
        finish_kernel,
        [VMEM] * 2,
        [(rows, QW)],
        [(rows, QW), pltpu.SemaphoreType.DMA((2 * KVH,))],
        out_spec=anywhere,
    )(done, returned)


def solution(mesh):
    in_specs = (
        P(("groups", "req"), None, None, None),
        P(("groups", "req"), None),
        P("groups"),
        P("groups"),
        P(("groups", "req")),
        P("groups"),
        P("groups"),
    )
    out_specs = P(("groups", "req"), None)
    return jax.shard_map(
        on_device, mesh=mesh, in_specs=in_specs, out_specs=out_specs, check_vma=False
    )
```

```python
import functools

import jax
import jax.numpy as jnp
from jax import lax
from jax.experimental import pallas as pl
from jax.experimental.pallas import tpu as pltpu
from jax.sharding import PartitionSpec as P

HD = 128
DRAFT = 4
PAGE = 128
R_DEV = 12
PPR = 3
QW = 4096
KVW = 512
KVH = KVW // HD
GRP = QW // KVW
LANES = 128
WIDE = QW // GRP + LANES
SPAN = R_DEV * GRP * DRAFT
SLOT = GRP * DRAFT
FIRST = 4
SECOND = R_DEV - FIRST
BODY = 2
ROOM = 48
BF = jnp.bfloat16
F32 = jnp.float32
I32 = jnp.int32
VMEM = pl.BlockSpec(memory_space=pltpu.VMEM)
SMEM = pl.BlockSpec(memory_space=pltpu.SMEM)


def iota(shape, dim):
    return lax.broadcasted_iota(I32, shape, dim)


def onehot(mask):
    return jnp.where(mask, jnp.float32(1), jnp.float32(0)).astype(BF)


def exact_dot(a, b):
    return jnp.dot(a, b, preferred_element_type=F32)


def stacked(value, cap):
    width = value.shape[1] // cap
    return jnp.concatenate([value[:, r * width : (r + 1) * width] for r in range(cap)], axis=0)


def wrapped(value, count):
    value = jnp.where(value < 0, value + count, value)
    return jnp.where(value >= count, value - count, value)


def peers_of(k, offs_ref, cap, sign, me, count):
    off = jnp.full(k.shape, offs_ref[0], I32)
    first = jnp.zeros(k.shape, I32)
    for i in range(1, offs_ref.shape[0]):
        off = jnp.where(k >= i * cap, offs_ref[i], off)
        first = jnp.where(k >= i * cap, i * cap, first)
    return wrapped(me + sign * off, count), k - first


def owner_row(index):
    return (index >> 5) * DRAFT + (index & (DRAFT - 1)), (index >> 2) & (GRP - 1)


def pack_kernel(
    count, cap, order_hbm, offs_hbm, rows_hbm, out_hbm, order_ref, offs_ref, rows_ref, stack_ref, pick_ref, out_ref, in_sems, out_sems
):
    reads = [
        pltpu.make_async_copy(src, dst, in_sems.at[i])
        for i, (src, dst) in enumerate([(order_hbm, order_ref), (offs_hbm, offs_ref), (rows_hbm, rows_ref)])
    ]
    for read in reads:
        read.start()
    rows = rows_ref.shape[0]
    step = 64
    me = lax.axis_index("req")
    gap = jnp.zeros((step - rows, WIDE), BF)
    for h in range(GRP):
        stack_ref[h * step + rows : (h + 1) * step, :] = gap
    for read in reads[:2]:
        read.wait()
    rest = jnp.full((1, step - rows), -1, I32)
    k = jnp.concatenate([order_ref[...], rest, order_ref[...], rest], axis=1)
    peer, place = peers_of(k, offs_ref, cap, -1, me, count)
    spot = peer * GRP + (iota((1, LANES), 1) >= step).astype(I32)
    spot = jnp.where(k < 0, -1, spot + place * (count * GRP))
    at = iota((cap * count * GRP, LANES), 0)
    for b in range(GRP * step // LANES):
        pick_ref[:, b * LANES : (b + 1) * LANES] = onehot(at - 2 * b == spot)
    reads[2].wait()
    for h in range(GRP):
        for g in range(KVH):
            c = (g * GRP + h) * HD
            stack_ref[h * step : h * step + rows, g * HD : (g + 1) * HD] = rows_ref[:, c : c + HD]
        c = QW + h * HD
        stack_ref[h * step : h * step + rows, KVH * HD :] = rows_ref[:, c : c + HD]
    writes = []
    for start in range(0, WIDE, 2 * LANES):
        size = min(2 * LANES, WIDE - start)
        chunk = exact_dot(pick_ref[...], stack_ref[:, start : start + size]).astype(BF)
        for r in range(cap):
            cols = pl.ds(r * WIDE + start, size)
            out_ref[:, r * WIDE + start : r * WIDE + start + size] = chunk[r * count * GRP : (r + 1) * count * GRP]
            writes.append(pltpu.make_async_copy(out_ref.at[:, cols], out_hbm.at[:, cols], out_sems.at[len(writes)]))
            writes[-1].start()
    for write in writes:
        write.wait()


def maps_kernel(
    count,
    cap,
    order_ref,
    offs_ref,
    moved_ref,
    lengths_ref,
    visit_ref,
    take_ref,
    give_ref,
    done_ref,
    limit_ref,
):
    me = lax.axis_index("req")
    moved = moved_ref[me]
    wide = cap * count * GRP
    row = iota((SLOT, wide), 0)
    spot = jnp.zeros((SLOT, wide), I32)
    for t in range(DRAFT):
        k = moved * DRAFT + t
        c = k // cap
        peer = wrapped(me + offs_ref[c], count)
        spot = jnp.where((row & (DRAFT - 1)) == t, (k - c * cap) * (count * GRP) + peer * GRP, spot)
    visit_ref[...] = onehot(iota((SLOT, wide), 1) == spot + (row >> 2))
    row = iota((SPAN, LANES), 0)
    lane = iota((SPAN, LANES), 1)
    k, h = owner_row(row)
    peer, place = peers_of(k, offs_ref, cap, 1, me, count)
    spot = place * (count * GRP) + peer * GRP + h
    for b in range(wide // LANES):
        take_ref[:, b * LANES : (b + 1) * LANES] = onehot(spot - b * LANES == lane)
    lane = iota((1, SPAN), 1)
    k, h = owner_row(lane)
    peer, place = peers_of(k, offs_ref, cap, 1, me, count)
    spot = place * (count * GRP) + peer * GRP + h
    at = iota((wide, SPAN), 0)
    give_ref[:, :SPAN] = onehot(at == jnp.where((lane >> 5) == moved, -1, spot))
    lane = iota((1, SLOT), 1)
    spot = jnp.full((1, SLOT), 0, I32)
    for t in range(DRAFT):
        k = moved * DRAFT + t
        c = k // cap
        peer = wrapped(me + offs_ref[c], count)
        spot = jnp.where((lane & (DRAFT - 1)) == t, (k - c * cap) * (count * GRP) + peer * GRP, spot)
    give_ref[:, SPAN:] = onehot(iota((wide, SLOT), 0) == spot + (lane >> 2))
    rows = order_ref.shape[1]
    peer, place = peers_of(order_ref[...], offs_ref, cap, -1, me, count)
    spot = place * (count * GRP) + peer * GRP
    same = iota((rows, rows), 0) == iota((rows, rows), 1)
    spot = jnp.sum(jnp.where(same, spot, 0).astype(F32), axis=1, keepdims=True).astype(I32)
    lane = iota((rows, wide), 1)
    for h in range(GRP):
        done_ref[h * rows : (h + 1) * rows, :] = onehot(lane == spot + h)
    row = iota((16, LANES), 0)
    limit = jnp.full((16, LANES), moved, I32)
    limit = jnp.where(row == R_DEV + 1, lengths_ref[me * R_DEV + moved], limit)
    for s in range(R_DEV):
        limit = jnp.where(row == s, lengths_ref[me * R_DEV + s], limit)
    limit_ref[...] = limit


def visitor_kernel(count, cap, visit_ref, in_ref, out_ref):
    out_ref[...] = exact_dot(visit_ref[...], stacked(in_ref[...], cap)).astype(BF)


def attend(slots, rows_of, pages_of, limit_of, put, score_ref, weight_ref, inverse_ref):
    span = PPR * PAGE
    fresh = KVH * DRAFT
    two = 2 * SLOT
    scale = jnp.float32(HD**-0.5 * 1.4426950408889634)
    low = jnp.float32(-1e30)
    position = iota((1, span), 1)
    lane = iota((two, fresh), 1)
    row = iota((two, fresh), 0)
    seen = jnp.where((lane & (DRAFT - 1)) <= (row & (DRAFT - 1)), (lane >> 2) - (row >> 5), -1)
    blank = jnp.zeros((SLOT, HD), BF)
    units = [(s, g) for s in slots for g in range(0, KVH, 2)]

    def pair(s, g, kind):
        new = rows_of(s)[kind * fresh : (kind + 1) * fresh, KVW:]
        pages = [pages_of(s, p, kind, slice(g * HD, (g + 2) * HD)) for p in range(PPR)]
        return jnp.concatenate(pages + [jnp.concatenate([new, new], axis=1)], axis=0)

    def score(u):
        s, g = units[u]
        rows = rows_of(s)
        first = jnp.concatenate([rows[:, g * HD : (g + 1) * HD], blank], axis=1)
        second = jnp.concatenate([blank, rows[:, (g + 1) * HD : (g + 2) * HD]], axis=1)
        score_ref[u, :, : span + fresh] = lax.dot_general(
            jnp.concatenate([first, second], axis=0),
            pair(s, g, 0),
            (((1,), (1,)), ((), ())),
            preferred_element_type=F32,
        )

    def weigh(u):
        s, g = units[u]
        limit = jnp.concatenate([limit_of(s)] * (span // LANES), axis=1)
        old = jnp.where(position < limit, score_ref[u, :, :span], low)
        new = jnp.where(seen == g, score_ref[u, :, span : span + fresh], low)
        peak = jnp.maximum(jnp.max(old, axis=1, keepdims=True), jnp.max(new, axis=1, keepdims=True))
        old = jnp.exp2((old - peak) * scale)
        new = jnp.exp2((new - peak) * scale)
        total = jnp.sum(old, axis=1, keepdims=True) + jnp.sum(new, axis=1, keepdims=True)
        weight_ref[u, :, :span] = old.astype(BF)
        weight_ref[u, :, span : span + fresh] = new.astype(BF)
        inverse_ref[u] = jnp.broadcast_to(1.0 / total, (two, HD))

    def combine(u):
        s, g = units[u]
        summed = exact_dot(weight_ref[u, :, : span + fresh], pair(s, g, 1))
        for i in range(2):
            part = slice(i * SLOT, (i + 1) * SLOT)
            put(s, g + i, (summed[part, i * HD : (i + 1) * HD] * inverse_ref[u, part, :]).astype(BF))

    for stage in (score, weigh, combine):
        for u in range(len(units)):
            stage(u)


def attend_range(low, slots, rows_ref, cache_ref, limit_ref, out_ref, pages_ref, sems, *scratch):
    def step(i, carry):
        here = [i * BODY + j for j in range(BODY)]
        for s in here if sems is not None else []:
            fetch_pages(cache_ref, low, s, pages_ref, sems).wait()

        def put(s, g, value):
            out_ref[pl.ds(pl.multiple_of(s * SLOT, SLOT), SLOT), g * HD : (g + 1) * HD] = value

        attend(
            here,
            lambda s: rows_ref[pl.ds(pl.multiple_of((s + low) * SLOT, SLOT), SLOT), :],
            lambda s, p, kind, cols: pages_ref[s * PPR + p, kind, :, cols],
            lambda s: limit_ref[pl.ds(s + low, 1), :],
            put,
            *scratch,
        )
        return carry

    lax.fori_loop(0, slots // BODY, step, 0)


def fetch_pages(cache_ref, low, s, pages_ref, sems):
    return pltpu.make_async_copy(
        cache_ref.at[pl.ds((low + s) * PPR, PPR)], pages_ref.at[pl.ds(s * PPR, PPR)], sems.at[s]
    )


def first_kernel(
    count, cap, take_ref, limit_ref, in_ref, cache_ref, out_ref, rows_ref, guest_ref, sem, pages_ref, sems, *scratch
):
    for s in range(FIRST):
        fetch_pages(cache_ref, 0, s, pages_ref, sems).start()
    moved = jnp.max(limit_ref[R_DEV : R_DEV + 1, :])
    guest = pltpu.make_async_copy(cache_ref.at[pl.ds(moved * PPR, PPR)], guest_ref, sem)
    guest.start()
    rows_ref[...] = exact_dot(take_ref[...], stacked(in_ref[...], cap)).astype(BF)
    attend_range(0, FIRST, rows_ref, cache_ref, limit_ref, out_ref, pages_ref, sems, *scratch)
    guest.wait()


def second_kernel(count, cap, rows_ref, limit_ref, answer_ref, cache_ref, out_ref, *scratch):
    pages_ref = cache_ref.at[pl.ds(FIRST * PPR, SECOND * PPR)]
    attend_range(FIRST, SECOND, rows_ref, None, limit_ref, out_ref, pages_ref, None, *scratch)


def guest_kernel(count, cap, visitor_ref, limit_ref, pages_ref, out_ref, *scratch):
    def put(s, g, value):
        out_ref[:, g * HD : (g + 1) * HD] = value

    attend(
        [0],
        lambda s: visitor_ref[...],
        lambda s, p, kind, cols: pages_ref[p, kind, :, cols],
        lambda s: limit_ref[R_DEV + 1 : R_DEV + 2, :],
        put,
        *scratch,
    )


def reply_kernel(count, cap, give_ref, first_ref, second_ref, answer_ref, out_ref):
    rows = jnp.concatenate([first_ref[...], second_ref[...], answer_ref[...]], axis=0)
    sent = exact_dot(give_ref[...], rows).astype(BF)
    for r in range(cap):
        out_ref[:, r * KVW : (r + 1) * KVW] = sent[r * count * GRP : (r + 1) * count * GRP]


def finish_kernel(count, cap, done_ref, in_ref, out_hbm, out_ref, sems):
    rows = out_ref.shape[0]
    half = GRP // 2
    rhs = stacked(in_ref[...], cap)
    writes = []
    for i in range(2):
        result = exact_dot(done_ref[i * half * rows : (i + 1) * half * rows, :], rhs).astype(BF)
        for h in range(half):
            for g in range(KVH):
                c = (g * GRP + i * half + h) * HD
                out_ref[:, c : c + HD] = result[h * rows : (h + 1) * rows, g * HD : (g + 1) * HD]
        for g in range(KVH):
            cols = pl.ds((g * GRP + i * half) * HD, half * HD)
            writes.append(pltpu.make_async_copy(out_ref.at[:, cols], out_hbm.at[:, cols], sems.at[i * KVH + g]))
            writes[-1].start()
    for write in writes:
        write.wait()


def through_partner(mask, count, work, *args):
    def permuted(by, value):
        return lax.ppermute(value, "req", [(i, i ^ by) for i in range(count)])

    if count <= 16:
        branches = [
            functools.partial(lambda by, *a: work(functools.partial(permuted, by), *a), by) for by in range(1, count)
        ]
        return lax.switch(mask - 1, branches, *args)

    def swap(value):
        step = 1
        while step < count:
            choices = min(16, count // step)
            branches = [lambda v: v] + [functools.partial(permuted, d * step) for d in range(1, choices)]
            value = lax.switch(jnp.bitwise_and(mask // step, choices - 1), branches, value)
            step *= choices
        return value

    return work(swap, *args)


def on_device(kv_cache, draft_rows, cache_lengths, row_offsets, draft_order, pair_mask, moved_slots):
    count = lax.axis_size("req")
    rows = draft_rows.shape[0]
    cap = max(1, rows // count)
    order = draft_order.reshape(1, rows)
    mask = pair_mask[0]

    anywhere = pl.BlockSpec(memory_space=pl.ANY)

    def call(kernel, specs, outs, scratch=(), room=8, flops=10**8, out_spec=VMEM):
        outs = [o if isinstance(o, jax.ShapeDtypeStruct) else jax.ShapeDtypeStruct(o, BF) for o in outs]
        single = len(outs) == 1
        return pl.pallas_call(
            functools.partial(kernel, count, cap),
            in_specs=specs,
            out_specs=out_spec if single else [out_spec] * len(outs),
            out_shape=outs[0] if single else outs,
            scratch_shapes=[pltpu.VMEM(s, BF) if isinstance(s, tuple) else s for s in scratch],
            compiler_params=pltpu.CompilerParams(vmem_limit_bytes=room * 2**20),
            cost_estimate=pl.CostEstimate(flops=flops, bytes_accessed=10**6, transcendentals=0),
        )

    wide = cap * count * GRP
    outgoing = call(
        pack_kernel,
        [anywhere] * 3,
        [(count * GRP, cap * WIDE)],
        [
            pltpu.VMEM((1, rows), I32),
            pltpu.SMEM(row_offsets.shape, I32),
            (rows, draft_rows.shape[1]),
            (GRP * 64, WIDE),
            (cap * count * GRP, GRP * 64),
            (count * GRP, cap * WIDE),
            pltpu.SemaphoreType.DMA((3,)),
            pltpu.SemaphoreType.DMA((cap * pl.cdiv(WIDE, 2 * LANES),)),
        ],
        room=56,
        out_spec=anywhere,
    )(order, row_offsets, draft_rows)
    incoming = lax.all_to_all(outgoing, "req", split_axis=0, concat_axis=0, tiled=True)
    visit, take, give, done, limit = call(
        maps_kernel,
        [VMEM, SMEM, SMEM, SMEM],
        [
            (SLOT, wide),
            (SPAN, wide),
            (wide, SPAN + SLOT),
            (GRP * rows, wide),
            jax.ShapeDtypeStruct((16, LANES), I32),
        ],
        room=20,
        flops=10**9,
    )(order, row_offsets, moved_slots, cache_lengths)
    visitor = call(visitor_kernel, [VMEM, VMEM], [(SLOT, WIDE)])(visit, incoming)
    def units(slots):
        return [
            pltpu.VMEM((slots * KVH // 2, 2 * SLOT, (PPR + 1) * PAGE), F32),
            pltpu.VMEM((slots * KVH // 2, 2 * SLOT, (PPR + 1) * PAGE), BF),
            pltpu.VMEM((slots * KVH // 2, 2 * SLOT, HD), F32),
        ]

    def pages(slots):
        return [(slots * PPR,) + kv_cache.shape[1:], pltpu.SemaphoreType.DMA((slots,))]

    def work(swap, visitor, take, give, limit, incoming, kv_cache):
        arrived = swap(visitor)
        first, owned, guest = call(
            first_kernel,
            [VMEM] * 3 + [anywhere],
            [(FIRST * SLOT, KVW), (SPAN, WIDE), (PPR,) + kv_cache.shape[1:]],
            [pltpu.SemaphoreType.DMA(())] + pages(FIRST) + units(BODY),
            room=ROOM,
            flops=2 * 10**9,
        )(take, limit, incoming, kv_cache)
        answer = call(guest_kernel, [VMEM] * 3, [(SLOT, KVW)], units(1), room=8)(arrived, limit, guest)
        second = call(
            second_kernel,
            [VMEM] * 4,
            [(SECOND * SLOT, KVW)],
            units(BODY),
            room=16,
            flops=2 * 10**9,
        )(owned, limit, answer, kv_cache)
        answer = swap(answer)
        return call(reply_kernel, [VMEM] * 4, [(count * GRP, cap * KVW)])(give, first, second, answer)

    backward = through_partner(mask, count, work, visitor, take, give, limit, incoming, kv_cache)
    returned = lax.all_to_all(backward, "req", split_axis=0, concat_axis=0, tiled=True)
    return call(
        finish_kernel,
        [VMEM] * 2,
        [(rows, QW)],
        [(rows, QW), pltpu.SemaphoreType.DMA((2 * KVH,))],
        out_spec=anywhere,
    )(done, returned)


def solution(mesh):
    in_specs = (
        P(("groups", "req"), None, None, None),
        P(("groups", "req"), None),
        P("groups"),
        P("groups"),
        P(("groups", "req")),
        P("groups"),
        P("groups"),
    )
    out_specs = P(("groups", "req"), None)
    return jax.shard_map(
        on_device, mesh=mesh, in_specs=in_specs, out_specs=out_specs, check_vma=False
    )
```

```python
import functools

import jax
import jax.numpy as jnp
from jax import lax
from jax.experimental import pallas as pl
from jax.experimental.pallas import tpu as pltpu
from jax.sharding import PartitionSpec as P

HD = 128
DRAFT = 4
PAGE = 128
R_DEV = 12
PPR = 3
QW = 4096
KVW = 512
KVH = KVW // HD
GRP = QW // KVW
LANES = 128
WIDE = QW // GRP + LANES
SPAN = R_DEV * GRP * DRAFT
SLOT = GRP * DRAFT
FIRST = 4
SECOND = R_DEV - FIRST
BODY = 2
ROOM = 48
BF = jnp.bfloat16
F32 = jnp.float32
I32 = jnp.int32
VMEM = pl.BlockSpec(memory_space=pltpu.VMEM)
SMEM = pl.BlockSpec(memory_space=pltpu.SMEM)


def iota(shape, dim):
    return lax.broadcasted_iota(I32, shape, dim)


def onehot(mask):
    return jnp.where(mask, jnp.float32(1), jnp.float32(0)).astype(BF)


def exact_dot(a, b):
    return jnp.dot(a, b, preferred_element_type=F32)


def stacked(value, cap):
    width = value.shape[1] // cap
    return jnp.concatenate([value[:, r * width : (r + 1) * width] for r in range(cap)], axis=0)


def wrapped(value, count):
    value = jnp.where(value < 0, value + count, value)
    return jnp.where(value >= count, value - count, value)


def peers_of(k, offs_ref, cap, sign, me, count):
    off = jnp.full(k.shape, offs_ref[0], I32)
    first = jnp.zeros(k.shape, I32)
    for i in range(1, offs_ref.shape[0]):
        off = jnp.where(k >= i * cap, offs_ref[i], off)
        first = jnp.where(k >= i * cap, i * cap, first)
    return wrapped(me + sign * off, count), k - first


def message_row(place, peer, h, count, cap):
    half = (h >> 2) * cap + place
    return (half >> 1) * (count * GRP) + peer * GRP + (half & 1) * (GRP // 2) + (h & (GRP // 2 - 1))


def owner_row(index):
    return (index >> 5) * DRAFT + (index & (DRAFT - 1)), (index >> 2) & (GRP - 1)


def pack_kernel(
    count, cap, order_hbm, offs_hbm, rows_hbm, out_hbm, order_ref, offs_ref, rows_ref, stack_ref, pick_ref, out_ref, in_sems, out_sems
):
    reads = [
        pltpu.make_async_copy(src, dst, in_sems.at[i])
        for i, (src, dst) in enumerate([(order_hbm, order_ref), (offs_hbm, offs_ref), (rows_hbm, rows_ref)])
    ]
    for read in reads:
        read.start()
    rows = rows_ref.shape[0]
    step = 64
    me = lax.axis_index("req")
    gap = jnp.zeros((step - rows, WIDE), BF)
    for h in range(GRP):
        stack_ref[h * step + rows : (h + 1) * step, :] = gap
    for read in reads[:2]:
        read.wait()
    rest = jnp.full((1, step - rows), -1, I32)
    k = jnp.concatenate([order_ref[...], rest, order_ref[...], rest], axis=1)
    peer, place = peers_of(k, offs_ref, cap, -1, me, count)
    odd = (iota((1, LANES), 1) >= step).astype(I32)
    at = iota((cap * count * GRP, LANES), 0)
    depth = GRP * step // 2
    for b in range(GRP * step // LANES):
        spot = jnp.where(k < 0, -1, message_row(place, peer, 2 * b + odd, count, cap))
        pick_ref[:, b * LANES : (b + 1) * LANES] = onehot(at == spot)
    reads[2].wait()
    for h in range(GRP):
        for g in range(KVH):
            c = (g * GRP + h) * HD
            stack_ref[h * step : h * step + rows, g * HD : (g + 1) * HD] = rows_ref[:, c : c + HD]
        c = QW + h * HD
        stack_ref[h * step : h * step + rows, KVH * HD :] = rows_ref[:, c : c + HD]
    writes = []
    for start in range(0, WIDE, 2 * LANES):
        size = min(2 * LANES, WIDE - start)
        tall = count * GRP
        edges = (cap + 1) // 2 * tall, cap // 2 * tall
        low = exact_dot(pick_ref[: edges[0], :depth], stack_ref[:depth, start : start + size])
        high = exact_dot(pick_ref[edges[1] :, depth:], stack_ref[depth:, start : start + size])
        for r in range(cap):
            cols = pl.ds(r * WIDE + start, size)
            parts = []
            if r * tall < edges[0]:
                parts.append(low[r * tall : (r + 1) * tall])
            if r * tall >= edges[1]:
                parts.append(high[r * tall - edges[1] : (r + 1) * tall - edges[1]])
            out_ref[:, r * WIDE + start : r * WIDE + start + size] = sum(parts[1:], parts[0]).astype(BF)
            writes.append(pltpu.make_async_copy(out_ref.at[:, cols], out_hbm.at[:, cols], out_sems.at[len(writes)]))
            writes[-1].start()
    for write in writes:
        write.wait()


def guest_rows(t, moved, offs_ref, cap, me, count):
    peer = jnp.zeros(t.shape, I32)
    place = jnp.zeros(t.shape, I32)
    for i in range(DRAFT):
        k = moved * DRAFT + i
        c = k // cap
        peer = jnp.where(t == i, wrapped(me + offs_ref[c], count), peer)
        place = jnp.where(t == i, k - c * cap, place)
    return peer, place


def maps_kernel(
    count,
    cap,
    order_ref,
    offs_ref,
    moved_ref,
    lengths_ref,
    visit_ref,
    take_ref,
    give_ref,
    done_ref,
    limit_ref,
):
    me = lax.axis_index("req")
    moved = moved_ref[me]
    wide = cap * count * GRP
    row = iota((SLOT, wide), 0)
    peer, place = guest_rows(row & (DRAFT - 1), moved, offs_ref, cap, me, count)
    spot = message_row(place, peer, row >> 2, count, cap)
    visit_ref[...] = onehot(iota((SLOT, wide), 1) == spot)
    row = iota((SPAN, LANES), 0)
    lane = iota((SPAN, LANES), 1)
    k, h = owner_row(row)
    peer, place = peers_of(k, offs_ref, cap, 1, me, count)
    spot = message_row(place, peer, h, count, cap)
    for b in range(wide // LANES):
        take_ref[:, b * LANES : (b + 1) * LANES] = onehot(spot - b * LANES == lane)
    lane = iota((1, SPAN), 1)
    k, h = owner_row(lane)
    peer, place = peers_of(k, offs_ref, cap, 1, me, count)
    spot = message_row(place, peer, h, count, cap)
    at = iota((wide, SPAN), 0)
    give_ref[:, :SPAN] = onehot(at == jnp.where((lane >> 5) == moved, -1, spot))
    lane = iota((1, SLOT), 1)
    peer, place = guest_rows(lane & (DRAFT - 1), moved, offs_ref, cap, me, count)
    give_ref[:, SPAN:] = onehot(iota((wide, SLOT), 0) == message_row(place, peer, lane >> 2, count, cap))
    rows = order_ref.shape[1]
    peer, place = peers_of(order_ref[...], offs_ref, cap, -1, me, count)
    same = iota((rows, rows), 0) == iota((rows, rows), 1)

    def upright(value):
        return jnp.sum(jnp.where(same, value, 0).astype(F32), axis=1, keepdims=True).astype(I32)

    lane = iota((rows, wide), 1)
    peer, place = upright(peer), upright(place)
    for h in range(GRP):
        done_ref[h * rows : (h + 1) * rows, :] = onehot(lane == message_row(place, peer, h, count, cap))
    row = iota((16, LANES), 0)
    limit = jnp.full((16, LANES), moved, I32)
    limit = jnp.where(row == R_DEV + 1, lengths_ref[me * R_DEV + moved], limit)
    for s in range(R_DEV):
        limit = jnp.where(row == s, lengths_ref[me * R_DEV + s], limit)
    limit_ref[...] = limit


def visitor_kernel(count, cap, visit_ref, in_ref, out_ref):
    out_ref[...] = exact_dot(visit_ref[...], stacked(in_ref[...], cap)).astype(BF)


def attend(slots, rows_of, pages_of, limit_of, put, score_ref, weight_ref, inverse_ref):
    span = PPR * PAGE
    fresh = KVH * DRAFT
    two = 2 * SLOT
    scale = jnp.float32(HD**-0.5 * 1.4426950408889634)
    low = jnp.float32(-1e30)
    position = iota((1, span), 1)
    lane = iota((two, fresh), 1)
    row = iota((two, fresh), 0)
    seen = jnp.where((lane & (DRAFT - 1)) <= (row & (DRAFT - 1)), (lane >> 2) - (row >> 5), -1)
    blank = jnp.zeros((SLOT, HD), BF)
    units = [(s, g) for s in slots for g in range(0, KVH, 2)]

    def pair(s, g, kind):
        new = rows_of(s)[kind * fresh : (kind + 1) * fresh, KVW:]
        pages = [pages_of(s, p, kind, slice(g * HD, (g + 2) * HD)) for p in range(PPR)]
        return jnp.concatenate(pages + [jnp.concatenate([new, new], axis=1)], axis=0)

    def score(u):
        s, g = units[u]
        rows = rows_of(s)
        first = jnp.concatenate([rows[:, g * HD : (g + 1) * HD], blank], axis=1)
        second = jnp.concatenate([blank, rows[:, (g + 1) * HD : (g + 2) * HD]], axis=1)
        score_ref[u, :, : span + fresh] = lax.dot_general(
            jnp.concatenate([first, second], axis=0),
            pair(s, g, 0),
            (((1,), (1,)), ((), ())),
            preferred_element_type=F32,
        )

    def weigh(u):
        s, g = units[u]
        limit = jnp.concatenate([limit_of(s)] * (span // LANES), axis=1)
        old = jnp.where(position < limit, score_ref[u, :, :span], low)
        new = jnp.where(seen == g, score_ref[u, :, span : span + fresh], low)
        peak = jnp.maximum(jnp.max(old, axis=1, keepdims=True), jnp.max(new, axis=1, keepdims=True))
        old = jnp.exp2((old - peak) * scale)
        new = jnp.exp2((new - peak) * scale)
        total = jnp.sum(old, axis=1, keepdims=True) + jnp.sum(new, axis=1, keepdims=True)
        weight_ref[u, :, :span] = old.astype(BF)
        weight_ref[u, :, span : span + fresh] = new.astype(BF)
        inverse_ref[u] = jnp.broadcast_to(1.0 / total, (two, HD))

    def combine(u):
        s, g = units[u]
        summed = exact_dot(weight_ref[u, :, : span + fresh], pair(s, g, 1))
        for i in range(2):
            part = slice(i * SLOT, (i + 1) * SLOT)
            put(s, g + i, (summed[part, i * HD : (i + 1) * HD] * inverse_ref[u, part, :]).astype(BF))

    for stage in (score, weigh, combine):
        for u in range(len(units)):
            stage(u)


def attend_range(low, slots, rows_ref, cache_ref, limit_ref, out_ref, pages_ref, sems, *scratch):
    def step(i, carry):
        here = [i * BODY + j for j in range(BODY)]
        for s in here if sems is not None else []:
            fetch_pages(cache_ref, low, s, pages_ref, sems).wait()

        def put(s, g, value):
            out_ref[pl.ds(pl.multiple_of(s * SLOT, SLOT), SLOT), g * HD : (g + 1) * HD] = value

        attend(
            here,
            lambda s: rows_ref[pl.ds(pl.multiple_of((s + low) * SLOT, SLOT), SLOT), :],
            lambda s, p, kind, cols: pages_ref[s * PPR + p, kind, :, cols],
            lambda s: limit_ref[pl.ds(s + low, 1), :],
            put,
            *scratch,
        )
        return carry

    lax.fori_loop(0, slots // BODY, step, 0)


def fetch_pages(cache_ref, low, s, pages_ref, sems):
    return pltpu.make_async_copy(
        cache_ref.at[pl.ds((low + s) * PPR, PPR)], pages_ref.at[pl.ds(s * PPR, PPR)], sems.at[s]
    )


def first_kernel(
    count, cap, take_ref, limit_ref, in_ref, cache_ref, out_ref, rows_ref, guest_ref, sem, pages_ref, sems, *scratch
):
    for s in range(FIRST):
        fetch_pages(cache_ref, 0, s, pages_ref, sems).start()
    moved = jnp.max(limit_ref[R_DEV : R_DEV + 1, :])
    guest = pltpu.make_async_copy(cache_ref.at[pl.ds(moved * PPR, PPR)], guest_ref, sem)
    guest.start()
    rows_ref[...] = exact_dot(take_ref[...], stacked(in_ref[...], cap)).astype(BF)
    attend_range(0, FIRST, rows_ref, cache_ref, limit_ref, out_ref, pages_ref, sems, *scratch)
    guest.wait()


def second_kernel(
    count, cap, give_ref, first_ref, rows_ref, limit_ref, answer_ref, cache_ref, out_ref, second_ref, *scratch
):
    pages_ref = cache_ref.at[pl.ds(FIRST * PPR, SECOND * PPR)]
    attend_range(FIRST, SECOND, rows_ref, None, limit_ref, second_ref, pages_ref, None, *scratch)
    sent = exact_dot(give_ref[:, :SPAN], jnp.concatenate([first_ref[...], second_ref[...]], axis=0)).astype(BF)
    for r in range(cap):
        out_ref[:, r * KVW : (r + 1) * KVW] = sent[r * count * GRP : (r + 1) * count * GRP]


def guest_kernel(count, cap, visitor_ref, limit_ref, pages_ref, out_ref, *scratch):
    def put(s, g, value):
        out_ref[:, g * HD : (g + 1) * HD] = value

    attend(
        [0],
        lambda s: visitor_ref[...],
        lambda s, p, kind, cols: pages_ref[p, kind, :, cols],
        lambda s: limit_ref[R_DEV + 1 : R_DEV + 2, :],
        put,
        *scratch,
    )


def reply_kernel(count, cap, give_ref, own_ref, answer_ref, out_ref):
    sent = exact_dot(give_ref[:, SPAN:], answer_ref[...]).astype(BF)
    for r in range(cap):
        cols = slice(r * KVW, (r + 1) * KVW)
        out_ref[:, cols] = own_ref[:, cols] + sent[r * count * GRP : (r + 1) * count * GRP]


def finish_kernel(count, cap, done_ref, in_ref, out_hbm, out_ref, sems):
    rows = out_ref.shape[0]
    half = GRP // 2
    arrived = stacked(in_ref[...], cap)
    tall = count * GRP
    spans = slice(0, (cap + 1) // 2 * tall), slice(cap // 2 * tall, cap * tall)
    writes = []
    for i, span in enumerate(spans):
        result = exact_dot(done_ref[i * half * rows : (i + 1) * half * rows, span], arrived[span]).astype(BF)
        for h in range(half):
            for g in range(KVH):
                c = (g * GRP + i * half + h) * HD
                out_ref[:, c : c + HD] = result[h * rows : (h + 1) * rows, g * HD : (g + 1) * HD]
        for g in range(KVH):
            cols = pl.ds((g * GRP + i * half) * HD, half * HD)
            writes.append(pltpu.make_async_copy(out_ref.at[:, cols], out_hbm.at[:, cols], sems.at[i * KVH + g]))
            writes[-1].start()
    for write in writes:
        write.wait()


def through_partner(mask, count, work, *args):
    def permuted(by, value):
        return lax.ppermute(value, "req", [(i, i ^ by) for i in range(count)])

    if count <= 16:
        branches = [
            functools.partial(lambda by, *a: work(functools.partial(permuted, by), *a), by) for by in range(1, count)
        ]
        return lax.switch(mask - 1, branches, *args)

    def swap(value):
        step = 1
        while step < count:
            choices = min(16, count // step)
            branches = [lambda v: v] + [functools.partial(permuted, d * step) for d in range(1, choices)]
            value = lax.switch(jnp.bitwise_and(mask // step, choices - 1), branches, value)
            step *= choices
        return value

    return work(swap, *args)


def on_device(kv_cache, draft_rows, cache_lengths, row_offsets, draft_order, pair_mask, moved_slots):
    count = lax.axis_size("req")
    rows = draft_rows.shape[0]
    cap = max(1, rows // count)
    order = draft_order.reshape(1, rows)
    mask = pair_mask[0]

    anywhere = pl.BlockSpec(memory_space=pl.ANY)

    def call(kernel, specs, outs, scratch=(), room=8, flops=10**8, out_spec=VMEM):
        outs = [o if isinstance(o, jax.ShapeDtypeStruct) else jax.ShapeDtypeStruct(o, BF) for o in outs]
        single = len(outs) == 1
        return pl.pallas_call(
            functools.partial(kernel, count, cap),
            in_specs=specs,
            out_specs=out_spec if single else [out_spec] * len(outs),
            out_shape=outs[0] if single else outs,
            scratch_shapes=[pltpu.VMEM(s, BF) if isinstance(s, tuple) else s for s in scratch],
            compiler_params=pltpu.CompilerParams(vmem_limit_bytes=room * 2**20),
            cost_estimate=pl.CostEstimate(flops=flops, bytes_accessed=10**6, transcendentals=0),
        )

    wide = cap * count * GRP
    outgoing = call(
        pack_kernel,
        [anywhere] * 3,
        [(count * GRP, cap * WIDE)],
        [
            pltpu.VMEM((1, rows), I32),
            pltpu.SMEM(row_offsets.shape, I32),
            (rows, draft_rows.shape[1]),
            (GRP * 64, WIDE),
            (cap * count * GRP, GRP * 64),
            (count * GRP, cap * WIDE),
            pltpu.SemaphoreType.DMA((3,)),
            pltpu.SemaphoreType.DMA((cap * pl.cdiv(WIDE, 2 * LANES),)),
        ],
        room=56,
        out_spec=anywhere,
    )(order, row_offsets, draft_rows)
    incoming = lax.all_to_all(outgoing, "req", split_axis=0, concat_axis=0, tiled=True)
    visit, take, give, done, limit = call(
        maps_kernel,
        [VMEM, SMEM, SMEM, SMEM],
        [
            (SLOT, wide),
            (SPAN, wide),
            (wide, SPAN + SLOT),
            (GRP * rows, wide),
            jax.ShapeDtypeStruct((16, LANES), I32),
        ],
        room=20,
        flops=10**9,
    )(order, row_offsets, moved_slots, cache_lengths)
    visitor = call(visitor_kernel, [VMEM, VMEM], [(SLOT, WIDE)])(visit, incoming)
    def units(slots):
        return [
            pltpu.VMEM((slots * KVH // 2, 2 * SLOT, (PPR + 1) * PAGE), F32),
            pltpu.VMEM((slots * KVH // 2, 2 * SLOT, (PPR + 1) * PAGE), BF),
            pltpu.VMEM((slots * KVH // 2, 2 * SLOT, HD), F32),
        ]

    def pages(slots):
        return [(slots * PPR,) + kv_cache.shape[1:], pltpu.SemaphoreType.DMA((slots,))]

    def work(swap, visitor, take, give, limit, incoming, kv_cache):
        arrived = swap(visitor)
        first, owned, guest = call(
            first_kernel,
            [VMEM] * 3 + [anywhere],
            [(FIRST * SLOT, KVW), (SPAN, WIDE), (PPR,) + kv_cache.shape[1:]],
            [pltpu.SemaphoreType.DMA(())] + pages(FIRST) + units(BODY),
            room=ROOM,
            flops=2 * 10**9,
        )(take, limit, incoming, kv_cache)
        answer = call(guest_kernel, [VMEM] * 3, [(SLOT, KVW)], units(1), room=8)(arrived, limit, guest)
        own = call(
            second_kernel,
            [VMEM] * 6,
            [(count * GRP, cap * KVW)],
            [(SECOND * SLOT, KVW)] + units(BODY),
            room=16,
            flops=2 * 10**9,
        )(give, first, owned, limit, answer, kv_cache)
        answer = swap(answer)
        return call(reply_kernel, [VMEM] * 3, [(count * GRP, cap * KVW)])(give, own, answer)

    backward = through_partner(mask, count, work, visitor, take, give, limit, incoming, kv_cache)
    returned = lax.all_to_all(backward, "req", split_axis=0, concat_axis=0, tiled=True)
    return call(
        finish_kernel,
        [VMEM] * 2,
        [(rows, QW)],
        [(rows, QW), pltpu.SemaphoreType.DMA((2 * KVH,))],
        out_spec=anywhere,
    )(done, returned)


def solution(mesh):
    in_specs = (
        P(("groups", "req"), None, None, None),
        P(("groups", "req"), None),
        P("groups"),
        P("groups"),
        P(("groups", "req")),
        P("groups"),
        P("groups"),
    )
    out_specs = P(("groups", "req"), None)
    return jax.shard_map(
        on_device, mesh=mesh, in_specs=in_specs, out_specs=out_specs, check_vma=False
    )
```

```python
import functools

import jax
import jax.numpy as jnp
from jax import lax
from jax.experimental import pallas as pl
from jax.experimental.pallas import tpu as pltpu
from jax.sharding import PartitionSpec as P

HD = 128
DRAFT = 4
PAGE = 128
R_DEV = 12
PPR = 3
QW = 4096
KVW = 512
KVH = KVW // HD
GRP = QW // KVW
LANES = 128
WIDE = QW // GRP + LANES
SPAN = R_DEV * GRP * DRAFT
SLOT = GRP * DRAFT
FIRST = 4
SECOND = R_DEV - FIRST
BODY = 2
ROOM = 48
BF = jnp.bfloat16
F32 = jnp.float32
I32 = jnp.int32
VMEM = pl.BlockSpec(memory_space=pltpu.VMEM)
SMEM = pl.BlockSpec(memory_space=pltpu.SMEM)


def iota(shape, dim):
    return lax.broadcasted_iota(I32, shape, dim)


def onehot(mask):
    return jnp.where(mask, jnp.float32(1), jnp.float32(0)).astype(BF)


def exact_dot(a, b):
    return jnp.dot(a, b, preferred_element_type=F32)


def stacked(value, cap):
    width = value.shape[1] // cap
    return jnp.concatenate([value[:, r * width : (r + 1) * width] for r in range(cap)], axis=0)


def wrapped(value, count):
    value = jnp.where(value < 0, value + count, value)
    return jnp.where(value >= count, value - count, value)


def peers_of(k, offs_ref, cap, sign, me, count):
    off = jnp.full(k.shape, offs_ref[0], I32)
    first = jnp.zeros(k.shape, I32)
    for i in range(1, offs_ref.shape[0]):
        off = jnp.where(k >= i * cap, offs_ref[i], off)
        first = jnp.where(k >= i * cap, i * cap, first)
    return wrapped(me + sign * off, count), k - first


def message_row(place, peer, h, count, cap):
    half = (h >> 2) * cap + place
    return (half >> 1) * (count * GRP) + peer * GRP + (half & 1) * (GRP // 2) + (h & (GRP // 2 - 1))


def owner_row(index):
    return (index >> 5) * DRAFT + (index & (DRAFT - 1)), (index >> 2) & (GRP - 1)


def pack_kernel(
    count, cap, order_hbm, offs_hbm, rows_hbm, out_hbm, order_ref, offs_ref, rows_ref, stack_ref, pick_ref, out_ref, in_sems, out_sems
):
    reads = [
        pltpu.make_async_copy(src, dst, in_sems.at[i])
        for i, (src, dst) in enumerate([(order_hbm, order_ref), (offs_hbm, offs_ref), (rows_hbm, rows_ref)])
    ]
    for read in reads:
        read.start()
    rows = rows_ref.shape[0]
    step = 64
    me = lax.axis_index("req")
    gap = jnp.zeros((step - rows, WIDE), BF)
    for h in range(GRP):
        stack_ref[h * step + rows : (h + 1) * step, :] = gap
    for read in reads[:2]:
        read.wait()
    rest = jnp.full((1, step - rows), -1, I32)
    k = jnp.concatenate([order_ref[...], rest, order_ref[...], rest], axis=1)
    peer, place = peers_of(k, offs_ref, cap, -1, me, count)
    odd = (iota((1, LANES), 1) >= step).astype(I32)
    at = iota((cap * count * GRP, LANES), 0)
    depth = GRP * step // 2
    for b in range(GRP * step // LANES):
        spot = jnp.where(k < 0, -1, message_row(place, peer, 2 * b + odd, count, cap))
        pick_ref[:, b * LANES : (b + 1) * LANES] = onehot(at == spot)
    reads[2].wait()
    for h in range(GRP):
        for g in range(KVH):
            c = (g * GRP + h) * HD
            stack_ref[h * step : h * step + rows, g * HD : (g + 1) * HD] = rows_ref[:, c : c + HD]
        c = QW + h * HD
        stack_ref[h * step : h * step + rows, KVH * HD :] = rows_ref[:, c : c + HD]
    writes = []
    for start in range(0, WIDE, 2 * LANES):
        size = min(2 * LANES, WIDE - start)
        tall = count * GRP
        edges = (cap + 1) // 2 * tall, cap // 2 * tall
        low = exact_dot(pick_ref[: edges[0], :depth], stack_ref[:depth, start : start + size])
        high = exact_dot(pick_ref[edges[1] :, depth:], stack_ref[depth:, start : start + size])
        for r in range(cap):
            cols = pl.ds(r * WIDE + start, size)
            parts = []
            if r * tall < edges[0]:
                parts.append(low[r * tall : (r + 1) * tall])
            if r * tall >= edges[1]:
                parts.append(high[r * tall - edges[1] : (r + 1) * tall - edges[1]])
            out_ref[:, r * WIDE + start : r * WIDE + start + size] = sum(parts[1:], parts[0]).astype(BF)
            writes.append(pltpu.make_async_copy(out_ref.at[:, cols], out_hbm.at[:, cols], out_sems.at[len(writes)]))
            writes[-1].start()
    for write in writes:
        write.wait()


def guest_rows(t, moved, offs_ref, cap, me, count):
    peer = jnp.zeros(t.shape, I32)
    place = jnp.zeros(t.shape, I32)
    for i in range(DRAFT):
        k = moved * DRAFT + i
        c = k // cap
        peer = jnp.where(t == i, wrapped(me + offs_ref[c], count), peer)
        place = jnp.where(t == i, k - c * cap, place)
    return peer, place


def maps_kernel(
    count,
    cap,
    order_ref,
    offs_ref,
    moved_ref,
    lengths_ref,
    visit_ref,
    take_ref,
    give_ref,
    done_ref,
    limit_ref,
):
    me = lax.axis_index("req")
    moved = moved_ref[me]
    wide = cap * count * GRP
    row = iota((SLOT, wide), 0)
    peer, place = guest_rows(row & (DRAFT - 1), moved, offs_ref, cap, me, count)
    spot = message_row(place, peer, row >> 2, count, cap)
    visit_ref[...] = onehot(iota((SLOT, wide), 1) == spot)
    row = iota((SPAN, LANES), 0)
    lane = iota((SPAN, LANES), 1)
    k, h = owner_row(row)
    peer, place = peers_of(k, offs_ref, cap, 1, me, count)
    spot = message_row(place, peer, h, count, cap)
    for b in range(wide // LANES):
        take_ref[:, b * LANES : (b + 1) * LANES] = onehot(spot - b * LANES == lane)
    lane = iota((1, SPAN), 1)
    k, h = owner_row(lane)
    peer, place = peers_of(k, offs_ref, cap, 1, me, count)
    spot = message_row(place, peer, h, count, cap)
    at = iota((wide, SPAN), 0)
    give_ref[:, :SPAN] = onehot(at == jnp.where((lane >> 5) == moved, -1, spot))
    lane = iota((1, SLOT), 1)
    peer, place = guest_rows(lane & (DRAFT - 1), moved, offs_ref, cap, me, count)
    give_ref[:, SPAN:] = onehot(iota((wide, SLOT), 0) == message_row(place, peer, lane >> 2, count, cap))
    rows = order_ref.shape[1]
    peer, place = peers_of(order_ref[...], offs_ref, cap, -1, me, count)
    same = iota((rows, rows), 0) == iota((rows, rows), 1)

    def upright(value):
        return jnp.sum(jnp.where(same, value, 0).astype(F32), axis=1, keepdims=True).astype(I32)

    lane = iota((rows, wide), 1)
    peer, place = upright(peer), upright(place)
    for h in range(GRP):
        done_ref[h * rows : (h + 1) * rows, :] = onehot(lane == message_row(place, peer, h, count, cap))
    row = iota((16, LANES), 0)
    limit = jnp.full((16, LANES), moved, I32)
    limit = jnp.where(row == R_DEV + 1, lengths_ref[me * R_DEV + moved], limit)
    for s in range(R_DEV):
        limit = jnp.where(row == s, lengths_ref[me * R_DEV + s], limit)
    limit_ref[...] = limit


def visitor_kernel(count, cap, visit_ref, in_ref, out_ref):
    out_ref[...] = exact_dot(visit_ref[...], stacked(in_ref[...], cap)).astype(BF)


def attend(slots, rows_of, pages_of, limit_of, put, score_ref, weight_ref, inverse_ref):
    span = PPR * PAGE
    fresh = KVH * DRAFT
    two = 2 * SLOT
    scale = jnp.float32(HD**-0.5 * 1.4426950408889634)
    low = jnp.float32(-3e38)
    position = iota((1, span), 1)
    lane = iota((two, fresh), 1)
    row = iota((two, fresh), 0)
    seen = jnp.where((lane & (DRAFT - 1)) <= (row & (DRAFT - 1)), (lane >> 2) - (row >> 5), -1)
    blank = jnp.zeros((SLOT, HD), BF)
    units = [(s, g) for s in slots for g in range(0, KVH, 2)]

    def pair(s, g, kind):
        new = rows_of(s)[kind * fresh : (kind + 1) * fresh, KVW:]
        pages = [pages_of(s, p, kind, slice(g * HD, (g + 2) * HD)) for p in range(PPR)]
        return jnp.concatenate(pages + [jnp.concatenate([new, new], axis=1)], axis=0)

    def score(u):
        s, g = units[u]
        rows = rows_of(s)
        first = jnp.concatenate([rows[:, g * HD : (g + 1) * HD], blank], axis=1)
        second = jnp.concatenate([blank, rows[:, (g + 1) * HD : (g + 2) * HD]], axis=1)
        score_ref[u, :, : span + fresh] = lax.dot_general(
            jnp.concatenate([first, second], axis=0),
            pair(s, g, 0),
            (((1,), (1,)), ((), ())),
            preferred_element_type=F32,
        )

    def weigh(u):
        s, g = units[u]
        limit = jnp.concatenate([limit_of(s)] * (span // LANES), axis=1)
        old = jnp.where(position < limit, score_ref[u, :, :span], low)
        new = jnp.where(seen == g, score_ref[u, :, span : span + fresh], low)
        peak = jnp.maximum(jnp.max(old, axis=1, keepdims=True), jnp.max(new, axis=1, keepdims=True))
        old = jnp.exp2((old - peak) * scale)
        new = jnp.exp2((new - peak) * scale)
        total = jnp.sum(old, axis=1, keepdims=True) + jnp.sum(new, axis=1, keepdims=True)
        weight_ref[u, :, :span] = old.astype(BF)
        weight_ref[u, :, span : span + fresh] = new.astype(BF)
        inverse_ref[u] = jnp.broadcast_to(1.0 / total, (two, HD))

    def combine(u):
        s, g = units[u]
        summed = exact_dot(weight_ref[u, :, : span + fresh], pair(s, g, 1))
        for i in range(2):
            part = slice(i * SLOT, (i + 1) * SLOT)
            put(s, g + i, (summed[part, i * HD : (i + 1) * HD] * inverse_ref[u, part, :]).astype(BF))

    for stage in (score, weigh, combine):
        for u in range(len(units)):
            stage(u)


def attend_range(low, slots, rows_ref, cache_ref, limit_ref, out_ref, pages_ref, sems, *scratch):
    def step(i, carry):
        here = [i * BODY + j for j in range(BODY)]
        for s in here if sems is not None else []:
            fetch_pages(cache_ref, low, s, pages_ref, sems).wait()

        def put(s, g, value):
            out_ref[pl.ds(pl.multiple_of(s * SLOT, SLOT), SLOT), g * HD : (g + 1) * HD] = value

        attend(
            here,
            lambda s: rows_ref[pl.ds(pl.multiple_of((s + low) * SLOT, SLOT), SLOT), :],
            lambda s, p, kind, cols: pages_ref[s * PPR + p, kind, :, cols],
            lambda s: limit_ref[pl.ds(s + low, 1), :],
            put,
            *scratch,
        )
        return carry

    lax.fori_loop(0, slots // BODY, step, 0)


def fetch_pages(cache_ref, low, s, pages_ref, sems):
    return pltpu.make_async_copy(
        cache_ref.at[pl.ds((low + s) * PPR, PPR)], pages_ref.at[pl.ds(s * PPR, PPR)], sems.at[s]
    )


def first_kernel(
    count, cap, take_ref, limit_ref, in_ref, cache_ref, out_ref, rows_ref, guest_ref, sem, pages_ref, sems, *scratch
):
    for s in range(FIRST):
        fetch_pages(cache_ref, 0, s, pages_ref, sems).start()
    moved = jnp.max(limit_ref[R_DEV : R_DEV + 1, :])
    guest = pltpu.make_async_copy(cache_ref.at[pl.ds(moved * PPR, PPR)], guest_ref, sem)
    guest.start()
    rows_ref[...] = exact_dot(take_ref[...], stacked(in_ref[...], cap)).astype(BF)
    attend_range(0, FIRST, rows_ref, cache_ref, limit_ref, out_ref, pages_ref, sems, *scratch)
    guest.wait()


def second_kernel(
    count, cap, give_ref, first_ref, rows_ref, limit_ref, answer_ref, cache_ref, out_ref, second_ref, *scratch
):
    pages_ref = cache_ref.at[pl.ds(FIRST * PPR, SECOND * PPR)]
    attend_range(FIRST, SECOND, rows_ref, None, limit_ref, second_ref, pages_ref, None, *scratch)
    sent = exact_dot(give_ref[:, :SPAN], jnp.concatenate([first_ref[...], second_ref[...]], axis=0)).astype(BF)
    for r in range(cap):
        out_ref[:, r * KVW : (r + 1) * KVW] = sent[r * count * GRP : (r + 1) * count * GRP]


def guest_kernel(count, cap, visitor_ref, limit_ref, pages_ref, out_ref, *scratch):
    def put(s, g, value):
        out_ref[:, g * HD : (g + 1) * HD] = value

    attend(
        [0],
        lambda s: visitor_ref[...],
        lambda s, p, kind, cols: pages_ref[p, kind, :, cols],
        lambda s: limit_ref[R_DEV + 1 : R_DEV + 2, :],
        put,
        *scratch,
    )


def reply_kernel(count, cap, give_ref, own_ref, answer_ref, out_ref):
    sent = exact_dot(give_ref[:, SPAN:], answer_ref[...]).astype(BF)
    for r in range(cap):
        cols = slice(r * KVW, (r + 1) * KVW)
        out_ref[:, cols] = own_ref[:, cols] + sent[r * count * GRP : (r + 1) * count * GRP]


def finish_kernel(count, cap, done_ref, in_ref, out_hbm, out_ref, sems):
    rows = out_ref.shape[0]
    half = GRP // 2
    arrived = stacked(in_ref[...], cap)
    tall = count * GRP
    spans = slice(0, (cap + 1) // 2 * tall), slice(cap // 2 * tall, cap * tall)
    writes = []
    for i, span in enumerate(spans):
        result = exact_dot(done_ref[i * half * rows : (i + 1) * half * rows, span], arrived[span]).astype(BF)
        for h in range(half):
            for g in range(KVH):
                c = (g * GRP + i * half + h) * HD
                out_ref[:, c : c + HD] = result[h * rows : (h + 1) * rows, g * HD : (g + 1) * HD]
        for g in range(KVH):
            cols = pl.ds((g * GRP + i * half) * HD, half * HD)
            writes.append(pltpu.make_async_copy(out_ref.at[:, cols], out_hbm.at[:, cols], sems.at[i * KVH + g]))
            writes[-1].start()
    for write in writes:
        write.wait()


def through_partner(mask, count, work, *args):
    def permuted(by, value):
        return lax.ppermute(value, "req", [(i, i ^ by) for i in range(count)])

    if count <= 16:
        branches = [
            functools.partial(lambda by, *a: work(functools.partial(permuted, by), *a), by) for by in range(1, count)
        ]
        return lax.switch(mask - 1, branches, *args)

    def swap(value):
        step = 1
        while step < count:
            choices = min(16, count // step)
            branches = [lambda v: v] + [functools.partial(permuted, d * step) for d in range(1, choices)]
            value = lax.switch(jnp.bitwise_and(mask // step, choices - 1), branches, value)
            step *= choices
        return value

    return work(swap, *args)


def on_device(kv_cache, draft_rows, cache_lengths, row_offsets, draft_order, pair_mask, moved_slots):
    count = lax.axis_size("req")
    rows = draft_rows.shape[0]
    cap = max(1, rows // count)
    order = draft_order.reshape(1, rows)
    mask = pair_mask[0]

    anywhere = pl.BlockSpec(memory_space=pl.ANY)

    def call(kernel, specs, outs, scratch=(), room=8, flops=10**8, out_spec=VMEM):
        outs = [o if isinstance(o, jax.ShapeDtypeStruct) else jax.ShapeDtypeStruct(o, BF) for o in outs]
        single = len(outs) == 1
        return pl.pallas_call(
            functools.partial(kernel, count, cap),
            in_specs=specs,
            out_specs=out_spec if single else [out_spec] * len(outs),
            out_shape=outs[0] if single else outs,
            scratch_shapes=[pltpu.VMEM(s, BF) if isinstance(s, tuple) else s for s in scratch],
            compiler_params=pltpu.CompilerParams(vmem_limit_bytes=room * 2**20),
            cost_estimate=pl.CostEstimate(flops=flops, bytes_accessed=10**6, transcendentals=0),
        )

    wide = cap * count * GRP
    outgoing = call(
        pack_kernel,
        [anywhere] * 3,
        [(count * GRP, cap * WIDE)],
        [
            pltpu.VMEM((1, rows), I32),
            pltpu.SMEM(row_offsets.shape, I32),
            (rows, draft_rows.shape[1]),
            (GRP * 64, WIDE),
            (cap * count * GRP, GRP * 64),
            (count * GRP, cap * WIDE),
            pltpu.SemaphoreType.DMA((3,)),
            pltpu.SemaphoreType.DMA((cap * pl.cdiv(WIDE, 2 * LANES),)),
        ],
        room=56,
        out_spec=anywhere,
    )(order, row_offsets, draft_rows)
    incoming = lax.all_to_all(outgoing, "req", split_axis=0, concat_axis=0, tiled=True)
    visit, take, give, done, limit = call(
        maps_kernel,
        [VMEM, SMEM, SMEM, SMEM],
        [
            (SLOT, wide),
            (SPAN, wide),
            (wide, SPAN + SLOT),
            (GRP * rows, wide),
            jax.ShapeDtypeStruct((16, LANES), I32),
        ],
        room=20,
        flops=10**9,
    )(order, row_offsets, moved_slots, cache_lengths)
    visitor = call(visitor_kernel, [VMEM, VMEM], [(SLOT, WIDE)])(visit, incoming)
    def units(slots):
        return [
            pltpu.VMEM((slots * KVH // 2, 2 * SLOT, (PPR + 1) * PAGE), F32),
            pltpu.VMEM((slots * KVH // 2, 2 * SLOT, (PPR + 1) * PAGE), BF),
            pltpu.VMEM((slots * KVH // 2, 2 * SLOT, HD), F32),
        ]

    def pages(slots):
        return [(slots * PPR,) + kv_cache.shape[1:], pltpu.SemaphoreType.DMA((slots,))]

    def work(swap, visitor, take, give, limit, incoming, kv_cache):
        arrived = swap(visitor)
        first, owned, guest = call(
            first_kernel,
            [VMEM] * 3 + [anywhere],
            [(FIRST * SLOT, KVW), (SPAN, WIDE), (PPR,) + kv_cache.shape[1:]],
            [pltpu.SemaphoreType.DMA(())] + pages(FIRST) + units(BODY),
            room=ROOM,
            flops=2 * 10**9,
        )(take, limit, incoming, kv_cache)
        answer = call(guest_kernel, [VMEM] * 3, [(SLOT, KVW)], units(1), room=8)(arrived, limit, guest)
        own = call(
            second_kernel,
            [VMEM] * 6,
            [(count * GRP, cap * KVW)],
            [(SECOND * SLOT, KVW)] + units(BODY),
            room=16,
            flops=2 * 10**9,
        )(give, first, owned, limit, answer, kv_cache)
        answer = swap(answer)
        return call(reply_kernel, [VMEM] * 3, [(count * GRP, cap * KVW)])(give, own, answer)

    backward = through_partner(mask, count, work, visitor, take, give, limit, incoming, kv_cache)
    returned = lax.all_to_all(backward, "req", split_axis=0, concat_axis=0, tiled=True)
    return call(
        finish_kernel,
        [VMEM] * 2,
        [(rows, QW)],
        [(rows, QW), pltpu.SemaphoreType.DMA((2 * KVH,))],
        out_spec=anywhere,
    )(done, returned)


def solution(mesh):
    in_specs = (
        P(("groups", "req"), None, None, None),
        P(("groups", "req"), None),
        P("groups"),
        P("groups"),
        P(("groups", "req")),
        P("groups"),
        P("groups"),
    )
    out_specs = P(("groups", "req"), None)
    return jax.shard_map(
        on_device, mesh=mesh, in_specs=in_specs, out_specs=out_specs, check_vma=False
    )
```

```python
import functools

import jax
import jax.numpy as jnp
from jax import lax
from jax.experimental import pallas as pl
from jax.experimental.pallas import tpu as pltpu
from jax.sharding import PartitionSpec as P

HD = 128
DRAFT = 4
PAGE = 128
R_DEV = 12
PPR = 3
QW = 4096
KVW = 512
KVH = KVW // HD
GRP = QW // KVW
LANES = 128
WIDE = QW // GRP + LANES
SPAN = R_DEV * GRP * DRAFT
SLOT = GRP * DRAFT
FIRST = 4
SECOND = R_DEV - FIRST
BODY = 2
ROOM = 48
BF = jnp.bfloat16
F32 = jnp.float32
I32 = jnp.int32
VMEM = pl.BlockSpec(memory_space=pltpu.VMEM)
SMEM = pl.BlockSpec(memory_space=pltpu.SMEM)


def iota(shape, dim):
    return lax.broadcasted_iota(I32, shape, dim)


def onehot(mask):
    return jnp.where(mask, jnp.float32(1), jnp.float32(0)).astype(BF)


def exact_dot(a, b):
    return jnp.dot(a, b, preferred_element_type=F32)


def stacked(value, cap):
    width = value.shape[1] // cap
    return jnp.concatenate([value[:, r * width : (r + 1) * width] for r in range(cap)], axis=0)


def wrapped(value, count):
    value = jnp.where(value < 0, value + count, value)
    return jnp.where(value >= count, value - count, value)


def peers_of(k, offs_ref, cap, sign, me, count):
    off = jnp.full(k.shape, offs_ref[0], I32)
    first = jnp.zeros(k.shape, I32)
    for i in range(1, offs_ref.shape[0]):
        off = jnp.where(k >= i * cap, offs_ref[i], off)
        first = jnp.where(k >= i * cap, i * cap, first)
    return wrapped(me + sign * off, count), k - first


def message_row(place, peer, h, count, cap):
    half = (h >> 2) * cap + place
    return (half >> 1) * (count * GRP) + peer * GRP + (half & 1) * (GRP // 2) + (h & (GRP // 2 - 1))


def owner_row(index):
    return (index >> 5) * DRAFT + (index & (DRAFT - 1)), (index >> 2) & (GRP - 1)


def pack_kernel(
    count, cap, order_hbm, offs_hbm, rows_hbm, out_hbm, order_ref, offs_ref, rows_ref, stack_ref, pick_ref, out_ref, in_sems, out_sems
):
    reads = [
        pltpu.make_async_copy(src, dst, in_sems.at[i])
        for i, (src, dst) in enumerate([(order_hbm, order_ref), (offs_hbm, offs_ref), (rows_hbm, rows_ref)])
    ]
    for read in reads:
        read.start()
    rows = rows_ref.shape[0]
    step = 64
    me = lax.axis_index("req")
    gap = jnp.zeros((step - rows, WIDE), BF)
    for h in range(GRP):
        stack_ref[h * step + rows : (h + 1) * step, :] = gap
    for read in reads[:2]:
        read.wait()
    rest = jnp.full((1, step - rows), -1, I32)
    k = jnp.concatenate([order_ref[...], rest, order_ref[...], rest], axis=1)
    peer, place = peers_of(k, offs_ref, cap, -1, me, count)
    odd = (iota((1, LANES), 1) >= step).astype(I32)
    depth = GRP * step // 2
    tall = count * GRP
    edges = (cap + 1) // 2 * tall, cap // 2 * tall
    for b in range(GRP * step // LANES):
        spot = jnp.where(k < 0, -1, message_row(place, peer, 2 * b + odd, count, cap))
        used = pl.ds(0, edges[0]) if b * LANES < depth else pl.ds(edges[1], cap * tall - edges[1])
        pick_ref[used, b * LANES : (b + 1) * LANES] = onehot(iota((used.size, LANES), 0) + used.start == spot)
    reads[2].wait()
    for h in range(GRP):
        for g in range(KVH):
            c = (g * GRP + h) * HD
            stack_ref[h * step : h * step + rows, g * HD : (g + 1) * HD] = rows_ref[:, c : c + HD]
        c = QW + h * HD
        stack_ref[h * step : h * step + rows, KVH * HD :] = rows_ref[:, c : c + HD]
    writes = []
    for start in range(0, WIDE, 2 * LANES):
        size = min(2 * LANES, WIDE - start)
        low = exact_dot(pick_ref[: edges[0], :depth], stack_ref[:depth, start : start + size])
        high = exact_dot(pick_ref[edges[1] :, depth:], stack_ref[depth:, start : start + size])
        for r in range(cap):
            cols = pl.ds(r * WIDE + start, size)
            parts = []
            if r * tall < edges[0]:
                parts.append(low[r * tall : (r + 1) * tall])
            if r * tall >= edges[1]:
                parts.append(high[r * tall - edges[1] : (r + 1) * tall - edges[1]])
            out_ref[:, r * WIDE + start : r * WIDE + start + size] = sum(parts[1:], parts[0]).astype(BF)
            writes.append(pltpu.make_async_copy(out_ref.at[:, cols], out_hbm.at[:, cols], out_sems.at[len(writes)]))
            writes[-1].start()
    for write in writes:
        write.wait()


def guest_rows(t, moved, offs_ref, cap, me, count):
    peer = jnp.zeros(t.shape, I32)
    place = jnp.zeros(t.shape, I32)
    for i in range(DRAFT):
        k = moved * DRAFT + i
        c = k // cap
        peer = jnp.where(t == i, wrapped(me + offs_ref[c], count), peer)
        place = jnp.where(t == i, k - c * cap, place)
    return peer, place


def maps_kernel(
    count,
    cap,
    order_ref,
    offs_ref,
    moved_ref,
    lengths_ref,
    visit_ref,
    take_ref,
    give_ref,
    done_ref,
    limit_ref,
):
    me = lax.axis_index("req")
    moved = moved_ref[me]
    wide = cap * count * GRP
    row = iota((SLOT, wide), 0)
    peer, place = guest_rows(row & (DRAFT - 1), moved, offs_ref, cap, me, count)
    spot = message_row(place, peer, row >> 2, count, cap)
    visit_ref[...] = onehot(iota((SLOT, wide), 1) == spot)
    row = iota((SPAN, LANES), 0)
    lane = iota((SPAN, LANES), 1)
    k, h = owner_row(row)
    peer, place = peers_of(k, offs_ref, cap, 1, me, count)
    spot = message_row(place, peer, h, count, cap)
    for b in range(wide // LANES):
        take_ref[:, b * LANES : (b + 1) * LANES] = onehot(spot - b * LANES == lane)
    lane = iota((1, SPAN), 1)
    k, h = owner_row(lane)
    peer, place = peers_of(k, offs_ref, cap, 1, me, count)
    spot = message_row(place, peer, h, count, cap)
    at = iota((wide, SPAN), 0)
    give_ref[:, :SPAN] = onehot(at == jnp.where((lane >> 5) == moved, -1, spot))
    lane = iota((1, SLOT), 1)
    peer, place = guest_rows(lane & (DRAFT - 1), moved, offs_ref, cap, me, count)
    give_ref[:, SPAN:] = onehot(iota((wide, SLOT), 0) == message_row(place, peer, lane >> 2, count, cap))
    rows = order_ref.shape[1]
    peer, place = peers_of(order_ref[...], offs_ref, cap, -1, me, count)
    same = iota((rows, rows), 0) == iota((rows, rows), 1)

    def upright(value):
        return jnp.sum(jnp.where(same, value, 0).astype(F32), axis=1, keepdims=True).astype(I32)

    lane = iota((rows, wide), 1)
    peer, place = upright(peer), upright(place)
    for h in range(GRP):
        done_ref[h * rows : (h + 1) * rows, :] = onehot(lane == message_row(place, peer, h, count, cap))
    row = iota((16, LANES), 0)
    limit = jnp.full((16, LANES), moved, I32)
    limit = jnp.where(row == R_DEV + 1, lengths_ref[me * R_DEV + moved], limit)
    for s in range(R_DEV):
        limit = jnp.where(row == s, lengths_ref[me * R_DEV + s], limit)
    limit_ref[...] = limit


def visitor_kernel(count, cap, visit_ref, in_ref, out_ref):
    out_ref[...] = exact_dot(visit_ref[...], stacked(in_ref[...], cap)).astype(BF)


def attend(slots, rows_of, pages_of, limit_of, put, score_ref, weight_ref, inverse_ref):
    span = PPR * PAGE
    fresh = KVH * DRAFT
    two = 2 * SLOT
    scale = jnp.float32(HD**-0.5 * 1.4426950408889634)
    low = jnp.float32(-3e38)
    position = iota((1, span), 1)
    lane = iota((two, fresh), 1)
    row = iota((two, fresh), 0)
    seen = jnp.where((lane & (DRAFT - 1)) <= (row & (DRAFT - 1)), (lane >> 2) - (row >> 5), -1)
    blank = jnp.zeros((SLOT, HD), BF)
    units = [(s, g) for s in slots for g in range(0, KVH, 2)]

    def pair(s, g, kind):
        new = rows_of(s)[kind * fresh : (kind + 1) * fresh, KVW:]
        pages = [pages_of(s, p, kind, slice(g * HD, (g + 2) * HD)) for p in range(PPR)]
        return jnp.concatenate(pages + [jnp.concatenate([new, new], axis=1)], axis=0)

    def score(u):
        s, g = units[u]
        rows = rows_of(s)
        first = jnp.concatenate([rows[:, g * HD : (g + 1) * HD], blank], axis=1)
        second = jnp.concatenate([blank, rows[:, (g + 1) * HD : (g + 2) * HD]], axis=1)
        score_ref[u, :, : span + fresh] = lax.dot_general(
            jnp.concatenate([first, second], axis=0),
            pair(s, g, 0),
            (((1,), (1,)), ((), ())),
            preferred_element_type=F32,
        )

    def weigh(u):
        s, g = units[u]
        limit = jnp.concatenate([limit_of(s)] * (span // LANES), axis=1)
        old = jnp.where(position < limit, score_ref[u, :, :span], low)
        new = jnp.where(seen == g, score_ref[u, :, span : span + fresh], low)
        peak = jnp.maximum(jnp.max(old, axis=1, keepdims=True), jnp.max(new, axis=1, keepdims=True))
        old = jnp.exp2((old - peak) * scale)
        new = jnp.exp2((new - peak) * scale)
        total = jnp.sum(old, axis=1, keepdims=True) + jnp.sum(new, axis=1, keepdims=True)
        weight_ref[u, :, :span] = old.astype(BF)
        weight_ref[u, :, span : span + fresh] = new.astype(BF)
        inverse_ref[u] = jnp.broadcast_to(1.0 / total, (two, HD))

    def combine(u):
        s, g = units[u]
        summed = exact_dot(weight_ref[u, :, : span + fresh], pair(s, g, 1))
        for i in range(2):
            part = slice(i * SLOT, (i + 1) * SLOT)
            put(s, g + i, (summed[part, i * HD : (i + 1) * HD] * inverse_ref[u, part, :]).astype(BF))

    for stage in (score, weigh, combine):
        for u in range(len(units)):
            stage(u)


def attend_range(low, slots, rows_ref, cache_ref, limit_ref, out_ref, pages_ref, sems, *scratch):
    def step(i, carry):
        here = [i * BODY + j for j in range(BODY)]
        for s in here if sems is not None else []:
            fetch_pages(cache_ref, low, s, pages_ref, sems).wait()

        def put(s, g, value):
            out_ref[pl.ds(pl.multiple_of(s * SLOT, SLOT), SLOT), g * HD : (g + 1) * HD] = value

        attend(
            here,
            lambda s: rows_ref[pl.ds(pl.multiple_of((s + low) * SLOT, SLOT), SLOT), :],
            lambda s, p, kind, cols: pages_ref[s * PPR + p, kind, :, cols],
            lambda s: limit_ref[pl.ds(s + low, 1), :],
            put,
            *scratch,
        )
        return carry

    lax.fori_loop(0, slots // BODY, step, 0)


def fetch_pages(cache_ref, low, s, pages_ref, sems):
    return pltpu.make_async_copy(
        cache_ref.at[pl.ds((low + s) * PPR, PPR)], pages_ref.at[pl.ds(s * PPR, PPR)], sems.at[s]
    )


def first_kernel(
    count, cap, take_ref, limit_ref, in_ref, cache_ref, out_ref, rows_ref, guest_ref, sem, pages_ref, sems, *scratch
):
    for s in range(FIRST):
        fetch_pages(cache_ref, 0, s, pages_ref, sems).start()
    moved = jnp.max(limit_ref[R_DEV : R_DEV + 1, :])
    guest = pltpu.make_async_copy(cache_ref.at[pl.ds(moved * PPR, PPR)], guest_ref, sem)
    guest.start()
    rows_ref[...] = exact_dot(take_ref[...], stacked(in_ref[...], cap)).astype(BF)
    attend_range(0, FIRST, rows_ref, cache_ref, limit_ref, out_ref, pages_ref, sems, *scratch)
    guest.wait()


def second_kernel(
    count, cap, give_ref, first_ref, rows_ref, limit_ref, answer_ref, cache_ref, out_ref, second_ref, *scratch
):
    pages_ref = cache_ref.at[pl.ds(FIRST * PPR, SECOND * PPR)]
    attend_range(FIRST, SECOND, rows_ref, None, limit_ref, second_ref, pages_ref, None, *scratch)
    sent = exact_dot(give_ref[:, :SPAN], jnp.concatenate([first_ref[...], second_ref[...]], axis=0)).astype(BF)
    for r in range(cap):
        out_ref[:, r * KVW : (r + 1) * KVW] = sent[r * count * GRP : (r + 1) * count * GRP]


def guest_kernel(count, cap, visitor_ref, limit_ref, pages_ref, out_ref, *scratch):
    def put(s, g, value):
        out_ref[:, g * HD : (g + 1) * HD] = value

    attend(
        [0],
        lambda s: visitor_ref[...],
        lambda s, p, kind, cols: pages_ref[p, kind, :, cols],
        lambda s: limit_ref[R_DEV + 1 : R_DEV + 2, :],
        put,
        *scratch,
    )


def reply_kernel(count, cap, give_ref, own_ref, answer_ref, out_ref):
    sent = exact_dot(give_ref[:, SPAN:], answer_ref[...]).astype(BF)
    for r in range(cap):
        cols = slice(r * KVW, (r + 1) * KVW)
        out_ref[:, cols] = own_ref[:, cols] + sent[r * count * GRP : (r + 1) * count * GRP]


def finish_kernel(count, cap, done_ref, in_ref, out_hbm, out_ref, sems):
    rows = out_ref.shape[0]
    half = GRP // 2
    arrived = stacked(in_ref[...], cap)
    tall = count * GRP
    spans = slice(0, (cap + 1) // 2 * tall), slice(cap // 2 * tall, cap * tall)
    writes = []
    for i, span in enumerate(spans):
        result = exact_dot(done_ref[i * half * rows : (i + 1) * half * rows, span], arrived[span]).astype(BF)
        for h in range(half):
            for g in range(KVH):
                c = (g * GRP + i * half + h) * HD
                out_ref[:, c : c + HD] = result[h * rows : (h + 1) * rows, g * HD : (g + 1) * HD]
        for g in range(KVH):
            cols = pl.ds((g * GRP + i * half) * HD, half * HD)
            writes.append(pltpu.make_async_copy(out_ref.at[:, cols], out_hbm.at[:, cols], sems.at[i * KVH + g]))
            writes[-1].start()
    for write in writes:
        write.wait()


def through_partner(mask, count, work, *args):
    def permuted(by, value):
        return lax.ppermute(value, "req", [(i, i ^ by) for i in range(count)])

    if count <= 16:
        branches = [
            functools.partial(lambda by, *a: work(functools.partial(permuted, by), *a), by) for by in range(1, count)
        ]
        return lax.switch(mask - 1, branches, *args)

    def swap(value):
        step = 1
        while step < count:
            choices = min(16, count // step)
            branches = [lambda v: v] + [functools.partial(permuted, d * step) for d in range(1, choices)]
            value = lax.switch(jnp.bitwise_and(mask // step, choices - 1), branches, value)
            step *= choices
        return value

    return work(swap, *args)


def on_device(kv_cache, draft_rows, cache_lengths, row_offsets, draft_order, pair_mask, moved_slots):
    count = lax.axis_size("req")
    rows = draft_rows.shape[0]
    cap = max(1, rows // count)
    order = draft_order.reshape(1, rows)
    mask = pair_mask[0]

    anywhere = pl.BlockSpec(memory_space=pl.ANY)

    def call(kernel, specs, outs, scratch=(), room=8, flops=10**8, out_spec=VMEM):
        outs = [o if isinstance(o, jax.ShapeDtypeStruct) else jax.ShapeDtypeStruct(o, BF) for o in outs]
        single = len(outs) == 1
        return pl.pallas_call(
            functools.partial(kernel, count, cap),
            in_specs=specs,
            out_specs=out_spec if single else [out_spec] * len(outs),
            out_shape=outs[0] if single else outs,
            scratch_shapes=[pltpu.VMEM(s, BF) if isinstance(s, tuple) else s for s in scratch],
            compiler_params=pltpu.CompilerParams(vmem_limit_bytes=room * 2**20),
            cost_estimate=pl.CostEstimate(flops=flops, bytes_accessed=10**6, transcendentals=0),
        )

    wide = cap * count * GRP
    outgoing = call(
        pack_kernel,
        [anywhere] * 3,
        [(count * GRP, cap * WIDE)],
        [
            pltpu.VMEM((1, rows), I32),
            pltpu.SMEM(row_offsets.shape, I32),
            (rows, draft_rows.shape[1]),
            (GRP * 64, WIDE),
            (cap * count * GRP, GRP * 64),
            (count * GRP, cap * WIDE),
            pltpu.SemaphoreType.DMA((3,)),
            pltpu.SemaphoreType.DMA((cap * pl.cdiv(WIDE, 2 * LANES),)),
        ],
        room=56,
        out_spec=anywhere,
    )(order, row_offsets, draft_rows)
    incoming = lax.all_to_all(outgoing, "req", split_axis=0, concat_axis=0, tiled=True)
    visit, take, give, done, limit = call(
        maps_kernel,
        [VMEM, SMEM, SMEM, SMEM],
        [
            (SLOT, wide),
            (SPAN, wide),
            (wide, SPAN + SLOT),
            (GRP * rows, wide),
            jax.ShapeDtypeStruct((16, LANES), I32),
        ],
        room=20,
        flops=10**9,
    )(order, row_offsets, moved_slots, cache_lengths)
    visitor = call(visitor_kernel, [VMEM, VMEM], [(SLOT, WIDE)])(visit, incoming)
    def units(slots):
        return [
            pltpu.VMEM((slots * KVH // 2, 2 * SLOT, (PPR + 1) * PAGE), F32),
            pltpu.VMEM((slots * KVH // 2, 2 * SLOT, (PPR + 1) * PAGE), BF),
            pltpu.VMEM((slots * KVH // 2, 2 * SLOT, HD), F32),
        ]

    def pages(slots):
        return [(slots * PPR,) + kv_cache.shape[1:], pltpu.SemaphoreType.DMA((slots,))]

    def work(swap, visitor, take, give, limit, incoming, kv_cache):
        arrived = swap(visitor)
        first, owned, guest = call(
            first_kernel,
            [VMEM] * 3 + [anywhere],
            [(FIRST * SLOT, KVW), (SPAN, WIDE), (PPR,) + kv_cache.shape[1:]],
            [pltpu.SemaphoreType.DMA(())] + pages(FIRST) + units(BODY),
            room=ROOM,
            flops=2 * 10**9,
        )(take, limit, incoming, kv_cache)
        answer = call(guest_kernel, [VMEM] * 3, [(SLOT, KVW)], units(1), room=8)(arrived, limit, guest)
        own = call(
            second_kernel,
            [VMEM] * 6,
            [(count * GRP, cap * KVW)],
            [(SECOND * SLOT, KVW)] + units(BODY),
            room=16,
            flops=2 * 10**9,
        )(give, first, owned, limit, answer, kv_cache)
        answer = swap(answer)
        return call(reply_kernel, [VMEM] * 3, [(count * GRP, cap * KVW)])(give, own, answer)

    backward = through_partner(mask, count, work, visitor, take, give, limit, incoming, kv_cache)
    returned = lax.all_to_all(backward, "req", split_axis=0, concat_axis=0, tiled=True)
    return call(
        finish_kernel,
        [VMEM] * 2,
        [(rows, QW)],
        [(rows, QW), pltpu.SemaphoreType.DMA((2 * KVH,))],
        out_spec=anywhere,
    )(done, returned)


def solution(mesh):
    in_specs = (
        P(("groups", "req"), None, None, None),
        P(("groups", "req"), None),
        P("groups"),
        P("groups"),
        P(("groups", "req")),
        P("groups"),
        P("groups"),
    )
    out_specs = P(("groups", "req"), None)
    return jax.shard_map(
        on_device, mesh=mesh, in_specs=in_specs, out_specs=out_specs, check_vma=False
    )
```
